256 devices in a mesh: scen: 4 (over y), fac: 64 (over z, x, core).
Axes of the slice: x: 4, y: 4, z: 8, core: 2. Of those that a mesh axis runs over, the one named last changes fastest.
Arguments:
- loadings: bfloat16 [65536, 1000], P('fac'), may hold values from -0.1875 to 0.1875
- reduced_shocks: bfloat16 [1000, 256], P(None, 'scen'), may hold values from -6 to 6
- sensitivity: bfloat16 [65536, 200], P('fac'), may hold values from -0.0234375 to 0.0234375
- cross_gamma: bfloat16 [128, 1024, 1024], P('fac'), may hold values from -0.005859375 to 0.005859375
- block_list: int32 [96, 3], replicated, may hold values from 0 to 199, as said below
- block_owner: int32 [96], replicated, may hold values from 0 to 63, as said below
- desk_owner: int32 [200], replicated, may hold values from 0 to 63, as said below
- buckets: int32 [65536], replicated, may hold values from 0 to 4
Outputs:
- desk_profit: float32 [320, 5, 256], P('fac', None, 'scen')
- shortfall: float32 [320, 5], P('fac')
- adjusted_es: float32 [320], P('fac')
The draws below stay inside these ranges and needn't reach their ends.
Inputs may be any that keep to these rules, and one draw needn't show every extreme that they name: `block_list`: each row is (row block, column block, desk): block numbers below 64, desks below 200; the fac index holding the row block, and the one holding the column block, is at most two away from the block's owner. `block_owner`: no fac index owns more than 2 blocks; some index owns exactly 2. `desk_owner`: no fac index owns more than 5 desks; some index owns exactly 5.
All inputs are finite; a program needn't handle non-finite values.
Results may differ from the reference program's by a relative error of at most 0.0032.
Values may be sent and summed in bfloat16 or wider, within the bound.
No kernel may reach another device: no remote copies, remote signals or barrier semaphores. Data moves between devices by JAX's collectives and lax.ppermute only.
A program may use at most 64 MiB of HBM per device.

```python
import jax
import jax.numpy as jnp
from jax import lax

K = 1000
BLK = 1024
DESKS = 200
HORIZONS = 5
F_DEV = 1024
CAP = 2
FACTORS = 65536
SCEN = 256
BLOCKS = 96
DESK_DEV = 5
DESK_SLOTS = 320
TAIL = 7
N_FAC = 64


def spread_owners(key, slots_each, chosen_count):
    subkeys = jax.random.split(key, 3)
    heavy_device = jax.random.randint(subkeys[0], (), 0, N_FAC)
    order_score = jax.random.permutation(subkeys[1], N_FAC * slots_each).astype(jnp.int32) + 1
    device_of = jnp.arange(N_FAC * slots_each, dtype=jnp.int32) // slots_each
    scores = jnp.where(device_of == heavy_device, 0, order_score)
    chosen = jnp.argsort(scores, stable=True)[:chosen_count]
    chosen = chosen[jax.random.permutation(subkeys[2], chosen_count)]
    return (chosen // slots_each).astype(jnp.int32)


def block_plan(key):
    base = jax.random.fold_in(key, 11)
    subkeys = jax.random.split(base, 6)
    owners = spread_owners(subkeys[0], CAP, BLOCKS)
    per_device = F_DEV // BLK
    row_device = jnp.clip(owners + jax.random.randint(subkeys[1], (BLOCKS,), -2, 3), 0, N_FAC - 1)
    col_device = jnp.clip(owners + jax.random.randint(subkeys[2], (BLOCKS,), -2, 3), 0, N_FAC - 1)
    row_block = row_device * per_device + jax.random.randint(subkeys[3], (BLOCKS,), 0, per_device)
    col_block = col_device * per_device + jax.random.randint(subkeys[4], (BLOCKS,), 0, per_device)
    desk_ids = jax.random.randint(subkeys[5], (BLOCKS,), 0, DESKS)
    listing = jnp.stack([row_block, col_block, desk_ids], axis=1).astype(jnp.int32)
    return (listing, owners)


def draw_block_list(key, part):
    return block_plan(key)[0]


def draw_block_owner(key, part):
    return block_plan(key)[1]


def draw_desk_owner(key, part):
    return spread_owners(jax.random.fold_in(key, 23), DESK_DEV, DESKS)


def plant(result, stream_key, low, high):
    place = [jax.random.randint(jax.random.fold_in(stream_key, axis), (), 0, length) for axis, length in enumerate(result.shape)]
    widest = result.shape.index(max(result.shape))
    beside = place[:widest] + [(place[widest] + 1) % result.shape[widest]] + place[widest + 1:]
    return result.at[tuple(place)].set(low).at[tuple(beside)].set(high)


def levels(key, extent, cuts, smallest, top_value):
    def one(axis_at, blocks):
        steps = jax.random.uniform(jax.random.fold_in(jax.random.fold_in(key, 6), axis_at), (blocks,), jnp.float32, smallest / len(cuts), top_value / len(cuts))
        return jnp.repeat(jnp.exp(steps), extent[axis_at] // blocks).reshape((-1,) + (1,) * (len(extent) - axis_at - 1))

    gain = one(*cuts[0])
    for cut in cuts[1:]:
        gain = gain * one(*cut)
    return gain


def noise(key, extent, deviation, reach, pieces=(), kind=jnp.bfloat16):
    drawn = deviation * jax.random.normal(key, extent, jnp.float32)
    if pieces:
        drawn = drawn * levels(key, extent, pieces, -0.22, 0.18)
    return jnp.clip(drawn, -reach, reach).astype(kind)


def setup_inputs(seed: int = 0) -> dict:
    streams_of = jax.random.split(jax.random.key(seed), 9)
    return {
        "loadings": noise(streams_of[0], (FACTORS, K), K ** -0.5, 0.1875, ((0, 64),)),
        "reduced_shocks": noise(streams_of[1], (K, SCEN), 1.0, 6.0, ((1, 4),)),
        "sensitivity": noise(streams_of[2], (FACTORS, DESKS), FACTORS ** -0.5, 0.0234375, ((0, 64),)),
        "cross_gamma": noise(streams_of[3], (N_FAC * CAP, BLK, BLK), (BLK * BLK) ** -0.5, 0.005859375, ((0, 64),)),
        "block_list": draw_block_list(jax.random.fold_in(streams_of[8], 71), 0),
        "block_owner": draw_block_owner(jax.random.fold_in(streams_of[8], 71), 0),
        "desk_owner": draw_desk_owner(jax.random.fold_in(streams_of[8], 71), 0),
        "buckets": plant(jax.random.randint(streams_of[7], (FACTORS,), 0, 5), jax.random.fold_in(streams_of[7], 1), 0, 4).astype(jnp.int32),
    }


horizon_weights = (1.0, 1.0, 2.0, 2.0, 6.0)

def owner_ranks(owners):
    position = jnp.arange(owners.shape[0], dtype=jnp.int32)
    same_owner = owners[:, None] == owners[None, :]
    earlier = position[None, :] < position[:, None]
    return lax.optimization_barrier(jnp.sum((same_owner & earlier).astype(jnp.int32), axis=1)).astype(jnp.int32)

def apply_masks(shocks, bucket_ids):
    horizon = jnp.arange(HORIZONS, dtype=jnp.int32)
    keeps_factor = bucket_ids[:, None] >= horizon[None, :]
    masked = jnp.where(keeps_factor[:, :, None], shocks[:, None, :], jnp.zeros((), jnp.bfloat16))
    return masked.reshape(shocks.shape[0], HORIZONS * shocks.shape[1])

def reference(loadings, reduced_shocks, sensitivity, cross_gamma, block_list, block_owner, desk_owner, buckets):
    shocks = jnp.dot(loadings, reduced_shocks, preferred_element_type=jnp.float32).astype(jnp.bfloat16)
    masked = apply_masks(shocks, buckets)
    total = lax.dot_general(sensitivity, masked, (((0,), (0,)), ((), ())), preferred_element_type=jnp.float32)
    block_slot = (block_owner * CAP + owner_ranks(block_owner)).astype(jnp.int32)
    desk_ids = jnp.arange(DESKS, dtype=jnp.int32)

    def add_block(block_index, running):
        block_entry = block_list[block_index]
        matrix = lax.dynamic_index_in_dim(cross_gamma, block_slot[block_index], 0, keepdims=False).astype(jnp.float32)
        row_part = lax.dynamic_slice_in_dim(masked, (block_entry[0] * BLK).astype(jnp.int32), BLK, 0)
        col_part = lax.dynamic_slice_in_dim(masked, (block_entry[1] * BLK).astype(jnp.int32), BLK, 0).astype(jnp.float32)
        product = jnp.dot(matrix, col_part, precision=lax.Precision.HIGHEST, preferred_element_type=jnp.float32)
        quad_term = 0.5 * lax.optimization_barrier(jnp.sum(row_part.astype(jnp.float32) * product, axis=0))
        return running + jnp.where((desk_ids == block_entry[2])[:, None], quad_term[None, :], jnp.zeros((), jnp.float32))
    total = lax.fori_loop(0, BLOCKS, add_block, total)
    desk_slot = (desk_owner * DESK_DEV + owner_ranks(desk_owner)).astype(jnp.int32)
    placement = (desk_slot[:, None] == jnp.arange(DESK_SLOTS, dtype=jnp.int32)[None, :]).astype(jnp.float32)
    profit = lax.dot_general(placement, total, (((0,), (0,)), ((), ())), precision=lax.Precision.HIGHEST, preferred_element_type=jnp.float32)
    profit = profit.reshape(DESK_SLOTS, HORIZONS, SCEN)
    worst_losses = lax.top_k(-profit, TAIL)[0]
    shortfall = lax.optimization_barrier(jnp.mean(worst_losses, axis=2))
    weights = jnp.array(horizon_weights, jnp.float32)
    adjusted = jnp.sqrt(lax.optimization_barrier(jnp.sum(weights[None, :] * shortfall * shortfall, axis=1)) + 1e-06)
    return (profit, shortfall, adjusted)
```

```python
import jax
import jax.numpy as jnp
from jax import lax
from jax.experimental import pallas as pl
from jax.experimental.pallas import tpu as pltpu
from jax.sharding import PartitionSpec as P

BLK = 1024
HORIZONS = 5
CAP = 2
DESK_DEV = 5
ROWS = 8
LANES = 256
TAIL = 7

horizon_weights = (1.0, 1.0, 2.0, 2.0, 6.0)


def swap_pairs(count):
    near, far, chip_near, chip_far = [], [], [], []
    for index in range(count):
        near.append((index, index ^ 1))
        other = ((index + 1) ^ 1) - 1
        if 0 <= other < count:
            far.append((index, other))
        chip, core = divmod(index, 2)
        chip_near.append((index, (chip ^ 1) * 2 + core))
        other = ((chip + 1) ^ 1) - 1
        if 0 <= other < count // 2:
            chip_far.append((index, other * 2 + core))
    return near, far, chip_near, chip_far


def shocks_kernel(loadings_t, reduced_t, shocks):
    shocks[...] = lax.dot_general(
        reduced_t[...], loadings_t[...], (((1,), (0,)), ((), ())), preferred_element_type=jnp.float32
    ).astype(jnp.bfloat16)


def lane_row(tile):
    return jnp.concatenate([tile[q : q + 1, :] for q in range(tile.shape[0])], axis=1)


def masked_rows(shocks, bucket_tile):
    bucket = jnp.broadcast_to(lane_row(bucket_tile), shocks.shape)
    value = shocks.astype(jnp.float32)
    pieces = [jnp.where(bucket >= h, value, 0.0) for h in range(HORIZONS)]
    return jnp.concatenate(pieces, axis=0).astype(jnp.bfloat16)


def packed_tail(tail):
    count = tail.shape[0]
    row = lax.broadcasted_iota(jnp.int32, (count, 64), 0) % ROWS
    pieces = []
    for q in range(4):
        piece = jnp.where(row == DESK_DEV, pltpu.roll(tail, DESK_DEV - q, 0), 0.0)
        if q == 0:
            piece = jnp.where(row == DESK_DEV + 1, pltpu.roll(tail, DESK_DEV - 3, 0), piece)
        pieces.append(piece)
    return jnp.concatenate(pieces, axis=1)


def delta_kernel(own, buckets, sens_t, owner_row_ref, out):
    desks = sens_t.shape[0]
    fac_count = out.shape[0]
    count = fac_count * ROWS
    device = lax.axis_index("fac")
    owner_row = owner_row_ref[...]
    groups = lax.broadcasted_iota(jnp.int32, (fac_count, desks), 0)
    member = jnp.where(groups == jnp.broadcast_to(owner_row, (fac_count, desks)), 1.0, 0.0)
    before = jnp.where(
        lax.broadcasted_iota(jnp.int32, (desks, desks), 0)
        < lax.broadcasted_iota(jnp.int32, (desks, desks), 1),
        1.0,
        0.0,
    )
    prefix = lax.dot_general(
        member.astype(jnp.bfloat16), before.astype(jnp.bfloat16), (((1,), (0,)), ((), ())),
        preferred_element_type=jnp.float32,
    )
    rank = jnp.sum(prefix * member, axis=0, keepdims=True).astype(jnp.int32)
    slot_row = owner_row * ROWS + rank
    placement = jnp.where(
        lax.broadcasted_iota(jnp.int32, (count, desks), 0)
        == jnp.broadcast_to(slot_row, (count, desks)),
        1.0,
        0.0,
    ).astype(jnp.bfloat16)
    placed = lax.dot_general(
        placement, sens_t[...], (((1,), (0,)), ((), ())), preferred_element_type=jnp.float32
    ).astype(jnp.bfloat16)
    masked = masked_rows(own[...], buckets[device])
    delta = lax.dot_general(
        placed, masked, (((1,), (1,)), ((), ())), preferred_element_type=jnp.float32
    )
    packed = delta[:, :LANES] + packed_tail(delta[:, LANES:])
    out[...] = packed.reshape(fac_count, ROWS, LANES)


def gamma_kernel(
    block_owner, block_list, desk_owner, own, near, far, chip_near, chip_far, buckets,
    owner_row_ref, gamma, delta, out,
):
    blocks = block_owner.shape[0]
    desks = desk_owner.shape[0]
    device = lax.axis_index("fac")
    live = jnp.int32(0)
    first = jnp.int32(0)
    second = jnp.int32(0)
    for block in reversed(range(blocks)):
        hit = block_owner[block] == device
        second = jnp.where(hit, first, second)
        first = jnp.where(hit, block, first)
        live = live + jnp.where(hit, 1, 0)
    core = device % 2
    chip = (device // 2) % 2
    out[...] = delta[...]
    width = HORIZONS * own.shape[0]

    def pick(block):
        offset = block - device
        towards = jnp.where(core == 0, offset, -offset)
        chip_towards = jnp.where(chip == 0, offset, -offset)
        code = jnp.where(
            offset == 0,
            0,
            jnp.where(
                jnp.abs(offset) == 1,
                jnp.where(towards > 0, 1, 2),
                jnp.where(chip_towards > 0, 3, 4),
            ),
        )
        value = own[...]
        for index, ref in ((1, near), (2, far), (3, chip_near), (4, chip_far)):
            value = jnp.where(code == index, ref[...], value)
        return masked_rows(value, buckets[block])

    for slot, block_index in enumerate((first, second)):
        @pl.when(slot < live)
        def _(slot=slot, block_index=block_index):
            row_part = pick(block_list[0, block_index])
            col_part = pick(block_list[1, block_index])
            desk = block_list[2, block_index]
            product = lax.dot_general(
                row_part, gamma[slot], (((1,), (0,)), ((), ())), preferred_element_type=jnp.float32
            )
            quad = 0.5 * jnp.sum(col_part.astype(jnp.float32) * product, axis=1, keepdims=True)
            diagonal = lax.broadcasted_iota(jnp.int32, (width, width), 0) == lax.broadcasted_iota(
                jnp.int32, (width, width), 1
            )
            quad_row = jnp.sum(
                jnp.where(diagonal, jnp.broadcast_to(quad, (width, width)), 0.0),
                axis=0,
                keepdims=True,
            )
            owner = desk_owner[desk]
            owner_row = owner_row_ref[...]
            earlier = jnp.logical_and(
                owner_row == owner, lax.broadcasted_iota(jnp.int32, (1, desks), 1) < desk
            )
            rank = jnp.sum(jnp.where(earlier, 1.0, 0.0)).astype(jnp.int32)
            tail = quad_row[:, LANES:]
            tail_row = jnp.concatenate([tail] * 4, axis=1)
            quarter = lax.broadcasted_iota(jnp.int32, (ROWS, LANES), 1) // 64
            row = lax.broadcasted_iota(jnp.int32, (ROWS, LANES), 0)
            addend = jnp.where(
                row == rank, jnp.broadcast_to(quad_row[:, :LANES], (ROWS, LANES)), 0.0
            )
            addend = addend + jnp.where(
                jnp.logical_and(row == DESK_DEV + rank // 4, quarter == rank % 4),
                jnp.broadcast_to(tail_row, (ROWS, LANES)),
                0.0,
            )
            out[owner] = out[owner] + addend


def sum_kernel(received, packed, profit):
    total = jnp.sum(received[...], axis=0)
    packed[...] = total
    for h in range(HORIZONS - 1):
        for j in range(DESK_DEV):
            profit[j, h : h + 1, :] = total[j : j + 1, 64 * h : 64 * h + 64]
    for j in range(DESK_DEV):
        row = DESK_DEV + j // 4
        profit[j, HORIZONS - 1 : HORIZONS, :] = total[row : row + 1, 64 * (j % 4) : 64 * (j % 4) + 64]


def tail_kernel(own, other1, other2, other3, shortfall, adjusted):
    parts = 4
    lanes = 128
    joined = -jnp.concatenate([own[...], other1[...], other2[...], other3[...]], axis=0)
    joined = jnp.concatenate([joined, jnp.zeros((lanes - parts * ROWS, LANES), jnp.float32)], axis=0)
    columns = jnp.transpose(joined)
    values = columns.reshape(4, 8, 8, lanes)
    lowest = -jnp.inf

    def across(value, op, axes):
        return op(value, axis=axes, keepdims=True)

    def over_parts(value, op):
        value = op(value, pltpu.roll(value, lanes - ROWS, 3))
        return op(value, pltpu.roll(value, lanes - 2 * ROWS, 3))

    lane = lax.broadcasted_iota(jnp.int32, (4, 1, 1, lanes), 3)

    def spread(value):
        value = jnp.where(lane < ROWS, value, 0.0)
        value = value + pltpu.roll(value, ROWS, 3)
        return value + pltpu.roll(value, 2 * ROWS, 3)

    total = jnp.zeros((4, 1, 1, lanes), jnp.float32)
    left = jnp.full((4, 1, 1, lanes), float(TAIL), jnp.float32)
    for _ in range(TAIL):
        best = jnp.max(jnp.max(values, axis=1, keepdims=True), axis=2, keepdims=True)
        best = spread(over_parts(best, jnp.maximum))
        same = values == jnp.broadcast_to(best, values.shape)
        count = jnp.sum(
            jnp.sum(jnp.where(same, 1.0, 0.0), axis=1, keepdims=True), axis=2, keepdims=True
        )
        count = over_parts(count, jnp.add)
        taken = jnp.minimum(count, left)
        total = total + jnp.where(taken > 0.0, taken * best, 0.0)
        left = left - taken
        values = jnp.where(same, lowest, values)
    mean = (total * (1.0 / TAIL)).reshape(4, lanes)
    square = jnp.concatenate([mean, jnp.zeros((lanes - 4, lanes), jnp.float32)], axis=0)
    flipped = jnp.transpose(square)[:ROWS, :]
    top = square[:ROWS, :]
    fifth = pltpu.roll(top, lanes - 1, 1)
    last = pltpu.roll(pltpu.roll(top, lanes - 2, 1), 4, 0)
    row = lax.broadcasted_iota(jnp.int32, (ROWS, lanes), 0)
    col = lax.broadcasted_iota(jnp.int32, (ROWS, lanes), 1)
    result = jnp.where(col < 4, flipped, jnp.where(row == 4, last, fifth))
    shortfall[...] = result[:DESK_DEV, :HORIZONS]
    weight = jnp.zeros((ROWS, lanes), jnp.float32)
    for h, value in enumerate(horizon_weights):
        weight = jnp.where(col == h, value, weight)
    used = jnp.where(jnp.logical_and(col < HORIZONS, row < DESK_DEV), result, 0.0)
    spent = jnp.sum(weight * used * used, axis=1, keepdims=True)
    diagonal = jnp.where(row == col, jnp.broadcast_to(spent, (ROWS, lanes)), 0.0)
    adjusted[...] = jnp.sqrt(jnp.sum(diagonal, axis=0, keepdims=True) + 1e-06)[:, :DESK_DEV]


VMEM = pl.BlockSpec(memory_space=pltpu.VMEM)
SMEM = pl.BlockSpec(memory_space=pltpu.SMEM)


def local(
    loadings, reduced_shocks, sensitivity, cross_gamma, block_list, block_owner, desk_owner, buckets
):
    fac_count = lax.axis_size("fac")
    scen_count = lax.axis_size("scen")
    s_dev = reduced_shocks.shape[1]
    f32 = jnp.float32
    shocks = pl.pallas_call(
        shocks_kernel,
        out_shape=jax.ShapeDtypeStruct((s_dev, BLK), jnp.bfloat16),
        in_specs=[VMEM, VMEM],
        out_specs=VMEM,
        name="shocks",
    )(loadings.T, reduced_shocks.T)
    moved = [lax.ppermute(shocks, "fac", pairs) for pairs in swap_pairs(fac_count)]
    tiles = buckets.reshape(fac_count, 8, 128)
    owner_row = desk_owner.reshape(1, -1)
    packed_shape = jax.ShapeDtypeStruct((fac_count, ROWS, LANES), f32)
    delta = pl.pallas_call(
        delta_kernel,
        out_shape=packed_shape,
        in_specs=[VMEM] * 4,
        out_specs=VMEM,
        name="delta",
    )(shocks, tiles, sensitivity.T, owner_row)
    terms = pl.pallas_call(
        gamma_kernel,
        out_shape=packed_shape,
        in_specs=[SMEM] * 3 + [VMEM] * 9,
        out_specs=VMEM,
        name="gamma",
    )(block_owner, block_list.T, desk_owner, shocks, *moved, tiles, owner_row, cross_gamma, delta)
    received = lax.all_to_all(terms, "fac", 0, 0, tiled=False)
    packed, profit = pl.pallas_call(
        sum_kernel,
        out_shape=(
            jax.ShapeDtypeStruct((ROWS, LANES), f32),
            jax.ShapeDtypeStruct((DESK_DEV, HORIZONS, s_dev), f32),
        ),
        in_specs=[VMEM],
        out_specs=(VMEM, VMEM),
        name="total",
    )(received)
    others = [
        lax.ppermute(packed, "scen", [(i, i ^ step) for i in range(scen_count)])
        for step in range(1, scen_count)
    ]
    shortfall, adjusted = pl.pallas_call(
        tail_kernel,
        out_shape=(
            jax.ShapeDtypeStruct((DESK_DEV, HORIZONS), f32),
            jax.ShapeDtypeStruct((1, DESK_DEV), f32),
        ),
        in_specs=[VMEM] * scen_count,
        out_specs=(VMEM, VMEM),
        name="tail",
    )(packed, *others)
    return (profit, shortfall, adjusted.reshape(DESK_DEV))


def solution(mesh):
    return jax.shard_map(
        local,
        mesh=mesh,
        in_specs=(
            P("fac", None),
            P(None, "scen"),
            P("fac", None),
            P("fac", None, None),
            P(),
            P(),
            P(),
            P(),
        ),
        out_specs=(P("fac", None, "scen"), P("fac", None), P("fac")),
        check_vma=False,
    )
```

```python
import jax
import jax.numpy as jnp
from jax import lax
from jax.experimental import pallas as pl
from jax.experimental.pallas import tpu as pltpu
from jax.sharding import PartitionSpec as P

BLK = 1024
HORIZONS = 5
CAP = 2
DESK_DEV = 5
ROWS = 8
LANES = 256
TAIL = 7
CHUNKS = 4

horizon_weights = (1.0, 1.0, 2.0, 2.0, 6.0)


def swap_pairs(count):
    near, far, chip_near, chip_far = [], [], [], []
    for index in range(count):
        near.append((index, index ^ 1))
        other = ((index + 1) ^ 1) - 1
        if 0 <= other < count:
            far.append((index, other))
        chip, core = divmod(index, 2)
        chip_near.append((index, (chip ^ 1) * 2 + core))
        other = ((chip + 1) ^ 1) - 1
        if 0 <= other < count // 2:
            chip_far.append((index, other * 2 + core))
    return near, far, chip_near, chip_far


def block_code(block, device):
    offset = block - device
    side = jnp.where(device % 2 == 0, offset, -offset)
    chip_side = jnp.where((device // 2) % 2 == 0, offset, -offset)
    beside = jnp.where(side > 0, 1, 2)
    apart = jnp.where(chip_side > 0, 3, 4)
    return jnp.where(offset == 0, 0, jnp.where(jnp.abs(offset) == 1, beside, apart))


def shocks_kernel(
    loadings_t, reduced_t, tiles_hbm, sens_hbm, owner_hbm, block_owner_hbm, block_list_hbm,
    desk_owner_hbm, shocks, tiles, sens_t, owner_row, meta, weights, factors, block_owner,
    block_list, desk_owner, sems,
):
    parts = CHUNKS
    span = BLK // parts
    copies = [pltpu.make_async_copy(reduced_t, factors, sems.at[parts])]
    for part in range(parts):
        window = pl.ds(part * span, span)
        copies.append(
            pltpu.make_async_copy(loadings_t.at[:, window], weights.at[:, window], sems.at[part])
        )
    scalars = [
        pltpu.make_async_copy(block_owner_hbm, block_owner, sems.at[parts + 1]),
        pltpu.make_async_copy(block_list_hbm, block_list, sems.at[parts + 2]),
        pltpu.make_async_copy(desk_owner_hbm, desk_owner, sems.at[parts + 3]),
    ]
    later = [
        pltpu.make_async_copy(owner_hbm, owner_row, sems.at[parts + 4]),
        pltpu.make_async_copy(tiles_hbm, tiles, sems.at[parts + 5]),
        pltpu.make_async_copy(sens_hbm, sens_t, sems.at[parts + 6]),
    ]
    for copy in scalars + copies + later:
        copy.start()
    for copy in scalars:
        copy.wait()
    device = lax.axis_index("fac")
    live = jnp.int32(0)
    first = jnp.int32(0)
    second = jnp.int32(0)
    for block in reversed(range(block_owner.shape[0])):
        hit = block_owner[block] == device
        second = jnp.where(hit, first, second)
        first = jnp.where(hit, block, first)
        live = live + jnp.where(hit, 1, 0)
    meta[0] = live
    for slot, block in enumerate((first, second)):
        row = block_list[0, block]
        col = block_list[1, block]
        desk = block_list[2, block]
        meta[1 + 6 * slot] = row
        meta[2 + 6 * slot] = block_code(row, device)
        meta[3 + 6 * slot] = col
        meta[4 + 6 * slot] = block_code(col, device)
        meta[5 + 6 * slot] = desk
        meta[6 + 6 * slot] = desk_owner[desk]
    copies[0].wait()
    for part in range(parts):
        copies[1 + part].wait()
        window = pl.ds(part * span, span)
        shocks[:, window] = lax.dot_general(
            factors[...], weights[:, window], (((1,), (0,)), ((), ())),
            preferred_element_type=jnp.float32,
        ).astype(jnp.bfloat16)
    for copy in later:
        copy.wait()


def lane_row(tile):
    return jnp.concatenate([tile[q : q + 1, :] for q in range(tile.shape[0])], axis=1)


def masked_rows(shocks, bucket_tile):
    bucket = jnp.broadcast_to(lane_row(bucket_tile), shocks.shape)
    value = shocks.astype(jnp.float32)
    pieces = [jnp.where(bucket >= h, value, 0.0) for h in range(HORIZONS)]
    return jnp.concatenate(pieces, axis=0).astype(jnp.bfloat16)


def packed_tail(tail):
    count = tail.shape[0]
    row = lax.broadcasted_iota(jnp.int32, (count, 64), 0) % ROWS
    pieces = []
    for q in range(4):
        piece = jnp.where(row == DESK_DEV, pltpu.roll(tail, DESK_DEV - q, 0), 0.0)
        if q == 0:
            piece = jnp.where(row == DESK_DEV + 1, pltpu.roll(tail, DESK_DEV - 3, 0), piece)
        pieces.append(piece)
    return jnp.concatenate(pieces, axis=1)


def encoded(chunks):
    largest = jnp.max(jnp.abs(chunks), axis=1, keepdims=True)
    exponent = jnp.ceil(jnp.log2(jnp.maximum(largest, 2.0**-100))) - 14.0
    shape = chunks.shape
    exponent = jnp.broadcast_to(exponent, shape)
    row = lax.broadcasted_iota(jnp.int32, shape, 1)
    value = jnp.where(row == ROWS - 1, exponent, jnp.round(chunks * jnp.exp2(-exponent)))
    value = jnp.concatenate([value[:, :, :128], value[:, :, 128:]], axis=1)
    return value.astype(jnp.int32).astype(jnp.int16)


def delta_kernel(own, buckets, sens_t, owner_row_ref, gamma_hbm, out, coded, gamma, sem):
    copy = pltpu.make_async_copy(gamma_hbm, gamma, sem)
    copy.start()
    desks = sens_t.shape[0]
    fac_count = out.shape[0]
    count = fac_count * ROWS
    device = lax.axis_index("fac")
    owner_row = owner_row_ref[...]
    groups = lax.broadcasted_iota(jnp.int32, (fac_count, desks), 0)
    member = jnp.where(groups == jnp.broadcast_to(owner_row, (fac_count, desks)), 1.0, 0.0)
    before = jnp.where(
        lax.broadcasted_iota(jnp.int32, (desks, desks), 0)
        < lax.broadcasted_iota(jnp.int32, (desks, desks), 1),
        1.0,
        0.0,
    )
    prefix = lax.dot_general(
        member.astype(jnp.bfloat16), before.astype(jnp.bfloat16), (((1,), (0,)), ((), ())),
        preferred_element_type=jnp.float32,
    )
    rank = jnp.sum(prefix * member, axis=0, keepdims=True).astype(jnp.int32)
    slot_row = owner_row * ROWS + rank
    placement = jnp.where(
        lax.broadcasted_iota(jnp.int32, (count, desks), 0)
        == jnp.broadcast_to(slot_row, (count, desks)),
        1.0,
        0.0,
    ).astype(jnp.bfloat16)
    placed = lax.dot_general(
        placement, sens_t[...], (((1,), (0,)), ((), ())), preferred_element_type=jnp.float32
    ).astype(jnp.bfloat16)
    masked = masked_rows(own[...], buckets[device])
    delta = lax.dot_general(
        placed, masked, (((1,), (1,)), ((), ())), preferred_element_type=jnp.float32
    )
    packed = delta[:, :LANES] + packed_tail(delta[:, LANES:])
    chunks = packed.reshape(fac_count, ROWS, LANES)
    out[...] = chunks
    coded[...] = encoded(chunks)
    copy.wait()


def gamma_kernel(
    meta, own, near, far, chip_near, chip_far, buckets, owner_row_ref, gamma, delta, coded, out, sums,
):
    del coded
    desks = owner_row_ref.shape[1]
    width = HORIZONS * own.shape[0]
    live = meta[0]
    sums[...] = jnp.zeros(sums.shape, jnp.float32)

    def pick(block, code):
        value = own[...]
        for index, ref in ((1, near), (2, far), (3, chip_near), (4, chip_far)):
            value = jnp.where(code == index, ref[...], value)
        return masked_rows(value, buckets[block])

    for slot in range(CAP):
        @pl.when(slot < live)
        def _(slot=slot):
            row_part = pick(meta[1 + 6 * slot], meta[2 + 6 * slot])
            col_part = pick(meta[3 + 6 * slot], meta[4 + 6 * slot])
            desk = meta[5 + 6 * slot]
            owner = meta[6 + 6 * slot]
            product = lax.dot_general(
                row_part, gamma[slot], (((1,), (0,)), ((), ())), preferred_element_type=jnp.float32
            )
            quad = 0.5 * jnp.sum(col_part.astype(jnp.float32) * product, axis=1, keepdims=True)
            diagonal = lax.broadcasted_iota(jnp.int32, (width, width), 0) == lax.broadcasted_iota(
                jnp.int32, (width, width), 1
            )
            quad_row = jnp.sum(
                jnp.where(diagonal, jnp.broadcast_to(quad, (width, width)), 0.0),
                axis=0,
                keepdims=True,
            )
            earlier = jnp.logical_and(
                owner_row_ref[...] == owner, lax.broadcasted_iota(jnp.int32, (1, desks), 1) < desk
            )
            rank = jnp.sum(jnp.where(earlier, 1.0, 0.0), axis=1, keepdims=True).astype(jnp.int32)
            rank = jnp.broadcast_to(rank, (ROWS, LANES))
            tail_row = jnp.concatenate([quad_row[:, LANES:]] * 4, axis=1)
            quarter = lax.broadcasted_iota(jnp.int32, (ROWS, LANES), 1) // 64
            row = lax.broadcasted_iota(jnp.int32, (ROWS, LANES), 0)
            moved = jnp.where(rank >= 4, 4, 0)
            in_tail = jnp.logical_and(
                row == DESK_DEV + jnp.where(rank >= 4, 1, 0), quarter == rank - moved
            )
            sums[slot] = jnp.where(
                row == rank,
                jnp.broadcast_to(quad_row[:, :LANES], (ROWS, LANES)),
                jnp.where(in_tail, jnp.broadcast_to(tail_row, (ROWS, LANES)), 0.0),
            )

    first = meta[6]
    second = jnp.where(live > 1, meta[12], first)
    joint = jnp.where(first == second, 1.0, 0.0)

    @pl.when(live > 0)
    def _():
        one = delta[first] + sums[0] + joint * sums[1]
        out[first] = encoded(one[None])[0]

    @pl.when(live > 1)
    def _():
        two = delta[second] + sums[1] + joint * sums[0]
        out[second] = encoded(two[None])[0]


def sum_kernel(received, packed, profit):
    lanes = 128
    value = received[...].astype(jnp.int32).astype(jnp.float32)
    value = value.reshape(received.shape[0] * 2, ROWS, lanes)
    scale = jnp.exp2(value[:, ROWS - 1 :, :])
    total = value * jnp.broadcast_to(scale, value.shape)
    total = jnp.sum(total.reshape(received.shape[0], 2, ROWS, lanes), axis=0)
    low, high = total[0], total[1]
    low_turned = pltpu.roll(low, 64, 1)
    high_turned = pltpu.roll(high, 64, 1)
    row = lax.broadcasted_iota(jnp.int32, (ROWS, lanes), 0)
    fifth = pltpu.roll(low, ROWS - DESK_DEV, 0)
    for j, source, shift in (
        (1, low_turned, 4), (2, high, 3), (3, high_turned, 2), (4, low, 2),
    ):
        moved = pltpu.roll(source, ROWS - shift, 0)
        fifth = jnp.where(row == j, moved, fifth)
    for h, block in enumerate((low, low_turned, high, high_turned, fifth)):
        packed[ROWS * h : ROWS * h + ROWS, :] = block
        for j in range(DESK_DEV):
            profit[j, h : h + 1, :] = block[j : j + 1, :64]


def tail_kernel(own, other1, other2, other3, shortfall, adjusted):
    lanes = 128
    count = HORIZONS * ROWS
    lane = lax.broadcasted_iota(jnp.int32, (count, lanes), 1)
    filler = jnp.zeros((lanes - count, lanes), jnp.float32)
    columns = []
    for one, two in ((own, other1), (other2, other3)):
        pair = -jnp.where(lane < 64, one[...], pltpu.roll(two[...], 64, 1))
        columns.append(jnp.transpose(jnp.concatenate([pair, filler], axis=0)))
    values = jnp.concatenate(columns, axis=0).reshape(32, 8, lanes)
    total = jnp.zeros((1, lanes), jnp.float32)
    left = jnp.full((1, lanes), float(TAIL), jnp.float32)
    for _ in range(TAIL):
        best = jnp.max(jnp.max(values, axis=0), axis=0, keepdims=True)
        same = values == jnp.broadcast_to(best[None], values.shape)
        found = jnp.sum(jnp.sum(jnp.where(same, 1.0, 0.0), axis=0), axis=0, keepdims=True)
        taken = jnp.minimum(found, left)
        total = total + jnp.where(taken > 0.0, taken * best, 0.0)
        left = left - taken
        values = jnp.where(same, -jnp.inf, values)
    mean = jnp.broadcast_to(total * (1.0 / TAIL), (ROWS, lanes))
    row = lax.broadcasted_iota(jnp.int32, (ROWS, lanes), 0)
    by_horizon = mean
    weight = jnp.full((ROWS, lanes), horizon_weights[0], jnp.float32)
    for h in range(1, HORIZONS):
        by_horizon = jnp.where(row == h, pltpu.roll(mean, lanes - ROWS * h, 1), by_horizon)
        weight = jnp.where(row == h, horizon_weights[h], weight)
    weight = jnp.where(row < HORIZONS, weight, 0.0)
    spent = jnp.sum(weight * by_horizon * by_horizon, axis=0, keepdims=True)
    adjusted[...] = jnp.sqrt(spent + 1e-06)[:, :DESK_DEV]
    square = jnp.concatenate([by_horizon, jnp.zeros((lanes - ROWS, lanes), jnp.float32)], axis=0)
    shortfall[...] = jnp.transpose(square)[:DESK_DEV, :HORIZONS]


VMEM = pl.BlockSpec(memory_space=pltpu.VMEM)
SMEM = pl.BlockSpec(memory_space=pltpu.SMEM)
HBM = pl.BlockSpec(memory_space=pltpu.HBM)
ORDER = (0, 2, 1, 3)


def held(value):
    return pltpu.with_memory_space_constraint(value, pltpu.VMEM)


def resident(value):
    return pltpu.with_memory_space_constraint(value, pltpu.HBM)


def limited(mib):
    return pltpu.CompilerParams(vmem_limit_bytes=mib << 20)


def local(
    loadings, reduced_shocks, sensitivity, cross_gamma, block_list, block_owner, desk_owner, buckets
):
    fac_count = lax.axis_size("fac")
    scen_count = lax.axis_size("scen")
    factors, s_dev = reduced_shocks.shape
    desks = desk_owner.shape[0]
    f32 = jnp.float32
    bf16 = jnp.bfloat16
    i32 = jnp.int32
    tile_shape = (fac_count, 8, BLK // 8)
    shocks, tiles, sens_t, owner_row, meta = pl.pallas_call(
        shocks_kernel,
        out_shape=(
            pltpu.VMEM((s_dev, BLK), bf16),
            pltpu.VMEM(tile_shape, i32),
            pltpu.VMEM((desks, BLK), bf16),
            pltpu.VMEM((1, desks), i32),
            pltpu.SMEM((16,), i32),
        ),
        in_specs=[HBM] * 8,
        out_specs=(VMEM, VMEM, VMEM, VMEM, SMEM),
        scratch_shapes=[
            pltpu.VMEM((factors, BLK), bf16),
            pltpu.VMEM((s_dev, factors), bf16),
            pltpu.SMEM(block_owner.shape, i32),
            pltpu.SMEM(block_list.shape[::-1], i32),
            pltpu.SMEM(desk_owner.shape, i32),
            pltpu.SemaphoreType.DMA((CHUNKS + 7,)),
        ],
        name="shocks",
        compiler_params=limited(10),
    )(
        *map(
            resident,
            (
                loadings.T, reduced_shocks.T, buckets.reshape(tile_shape), sensitivity.T,
                desk_owner.reshape(1, desks), block_owner, block_list.T, desk_owner,
            ),
        )
    )
    pairs = swap_pairs(fac_count)
    moved = {index: held(lax.ppermute(shocks, "fac", pairs[index])) for index in ORDER}
    chunk_shape = (fac_count, ROWS, LANES)
    coded_shape = pltpu.VMEM((fac_count, 2 * ROWS, LANES // 2), jnp.int16)
    delta, coded, gamma = pl.pallas_call(
        delta_kernel,
        out_shape=(
            pltpu.VMEM(chunk_shape, f32), coded_shape, pltpu.VMEM(cross_gamma.shape, bf16)
        ),
        in_specs=[VMEM] * 4 + [HBM],
        out_specs=(VMEM, VMEM, VMEM),
        scratch_shapes=[pltpu.SemaphoreType.DMA],
        name="delta",
        compiler_params=limited(16),
    )(shocks, tiles, sens_t, owner_row, resident(cross_gamma))
    terms = pl.pallas_call(
        gamma_kernel,
        out_shape=coded_shape,
        in_specs=[SMEM] + [VMEM] * 10,
        out_specs=VMEM,
        scratch_shapes=[pltpu.VMEM((CAP, ROWS, LANES), f32)],
        input_output_aliases={10: 0},
        name="gamma",
        compiler_params=limited(16),
    )(meta, shocks, moved[0], moved[1], moved[2], moved[3], tiles, owner_row, gamma, delta, coded)
    received = held(lax.all_to_all(terms, "fac", 0, 0, tiled=False))
    packed, profit = pl.pallas_call(
        sum_kernel,
        out_shape=(
            pltpu.VMEM((HORIZONS * ROWS, 128), f32),
            jax.ShapeDtypeStruct((DESK_DEV, HORIZONS, s_dev), f32),
        ),
        in_specs=[VMEM],
        out_specs=(VMEM, VMEM),
        name="total",
        compiler_params=limited(8),
    )(received)
    others = [
        held(lax.ppermute(packed, "scen", [(i, i ^ step) for i in range(scen_count)]))
        for step in (1, 3, 2)
    ]
    shortfall, adjusted = pl.pallas_call(
        tail_kernel,
        out_shape=(
            jax.ShapeDtypeStruct((DESK_DEV, HORIZONS), f32),
            jax.ShapeDtypeStruct((1, DESK_DEV), f32),
        ),
        in_specs=[VMEM] * scen_count,
        out_specs=(VMEM, VMEM),
        name="tail",
        compiler_params=limited(8),
    )(packed, *others)
    return (profit, shortfall, adjusted.reshape(DESK_DEV))


def solution(mesh):
    return jax.shard_map(
        local,
        mesh=mesh,
        in_specs=(
            P("fac", None),
            P(None, "scen"),
            P("fac", None),
            P("fac", None, None),
            P(),
            P(),
            P(),
            P(),
        ),
        out_specs=(P("fac", None, "scen"), P("fac", None), P("fac")),
        check_vma=False,
    )
```

```python
import jax
import jax.numpy as jnp
from jax import lax
from jax.experimental import pallas as pl
from jax.experimental.pallas import tpu as pltpu
from jax.sharding import PartitionSpec as P

BLK = 1024
HORIZONS = 5
CAP = 2
DESK_DEV = 5
ROWS = 8
LANES = 256
TAIL = 7
CHUNKS = 4

horizon_weights = (1.0, 1.0, 2.0, 2.0, 6.0)


def swap_pairs(count):
    near, far, chip_near, chip_far = [], [], [], []
    for index in range(count):
        near.append((index, index ^ 1))
        other = ((index + 1) ^ 1) - 1
        if 0 <= other < count:
            far.append((index, other))
        chip, core = divmod(index, 2)
        chip_near.append((index, (chip ^ 1) * 2 + core))
        other = ((chip + 1) ^ 1) - 1
        if 0 <= other < count // 2:
            chip_far.append((index, other * 2 + core))
    return near, far, chip_near, chip_far


def block_code(block, device):
    offset = block - device
    side = jnp.where(device % 2 == 0, offset, -offset)
    chip_side = jnp.where((device // 2) % 2 == 0, offset, -offset)
    beside = jnp.where(side > 0, 1, 2)
    apart = jnp.where(chip_side > 0, 3, 4)
    return jnp.where(offset == 0, 0, jnp.where(jnp.abs(offset) == 1, beside, apart))


def shocks_kernel(
    loadings_t, reduced_t, tiles_hbm, sens_hbm, owner_hbm, block_owner_hbm, block_list_hbm,
    desk_owner_hbm, shocks, tiles, sens_t, owner_row, meta, weights, factors, block_owner,
    block_list, desk_owner, sems,
):
    parts = CHUNKS
    span = BLK // parts
    copies = [pltpu.make_async_copy(reduced_t, factors, sems.at[parts])]
    for part in range(parts):
        window = pl.ds(part * span, span)
        copies.append(
            pltpu.make_async_copy(loadings_t.at[:, window], weights.at[:, window], sems.at[part])
        )
    scalars = [
        pltpu.make_async_copy(block_owner_hbm, block_owner, sems.at[parts + 1]),
        pltpu.make_async_copy(block_list_hbm, block_list, sems.at[parts + 2]),
        pltpu.make_async_copy(desk_owner_hbm, desk_owner, sems.at[parts + 3]),
    ]
    later = [
        pltpu.make_async_copy(owner_hbm, owner_row, sems.at[parts + 4]),
        pltpu.make_async_copy(tiles_hbm, tiles, sems.at[parts + 5]),
        pltpu.make_async_copy(sens_hbm, sens_t, sems.at[parts + 6]),
    ]
    for copy in scalars + copies + later:
        copy.start()
    for copy in scalars:
        copy.wait()
    device = lax.axis_index("fac")
    live = jnp.int32(0)
    first = jnp.int32(0)
    second = jnp.int32(0)
    for block in reversed(range(block_owner.shape[0])):
        hit = block_owner[block] == device
        second = jnp.where(hit, first, second)
        first = jnp.where(hit, block, first)
        live = live + jnp.where(hit, 1, 0)
    meta[0] = live
    for slot, block in enumerate((first, second)):
        row = block_list[0, block]
        col = block_list[1, block]
        desk = block_list[2, block]
        meta[1 + 6 * slot] = row
        meta[2 + 6 * slot] = block_code(row, device)
        meta[3 + 6 * slot] = col
        meta[4 + 6 * slot] = block_code(col, device)
        meta[5 + 6 * slot] = desk
        meta[6 + 6 * slot] = desk_owner[desk]
    copies[0].wait()
    for part in range(parts):
        copies[1 + part].wait()
        window = pl.ds(part * span, span)
        shocks[:, window] = lax.dot_general(
            factors[...], weights[:, window], (((1,), (0,)), ((), ())),
            preferred_element_type=jnp.float32,
        ).astype(jnp.bfloat16)
    for copy in later:
        copy.wait()


def lane_row(tile):
    return jnp.concatenate([tile[q : q + 1, :] for q in range(tile.shape[0])], axis=1)


def masked_rows(shocks, bucket_tile):
    bucket = jnp.broadcast_to(lane_row(bucket_tile), shocks.shape)
    value = shocks.astype(jnp.float32)
    pieces = [jnp.where(bucket >= h, value, 0.0) for h in range(HORIZONS)]
    return jnp.concatenate(pieces, axis=0).astype(jnp.bfloat16)


def packed_tail(tail):
    count = tail.shape[0]
    row = lax.broadcasted_iota(jnp.int32, (count, 64), 0) % ROWS
    pieces = []
    for q in range(4):
        piece = jnp.where(row == DESK_DEV, pltpu.roll(tail, DESK_DEV - q, 0), 0.0)
        if q == 0:
            piece = jnp.where(row == DESK_DEV + 1, pltpu.roll(tail, DESK_DEV - 3, 0), piece)
        pieces.append(piece)
    return jnp.concatenate(pieces, axis=1)


def encoded(chunks):
    largest = jnp.max(jnp.abs(chunks), axis=1, keepdims=True)
    exponent = jnp.ceil(jnp.log2(jnp.maximum(largest, 2.0**-100))) - 14.0
    shape = chunks.shape
    exponent = jnp.broadcast_to(exponent, shape)
    row = lax.broadcasted_iota(jnp.int32, shape, 1)
    value = jnp.where(row == ROWS - 1, exponent, jnp.round(chunks * jnp.exp2(-exponent)))
    value = jnp.concatenate([value[:, :, :128], value[:, :, 128:]], axis=1)
    return value.astype(jnp.int32).astype(jnp.int16)


def delta_kernel(own, buckets, sens_t, owner_row_ref, gamma_hbm, out, coded, gamma, sem):
    copy = pltpu.make_async_copy(gamma_hbm, gamma, sem)
    copy.start()
    desks = sens_t.shape[0]
    fac_count = out.shape[0]
    count = fac_count * ROWS
    device = lax.axis_index("fac")
    owner_row = owner_row_ref[...]
    groups = lax.broadcasted_iota(jnp.int32, (fac_count, desks), 0)
    member = jnp.where(groups == jnp.broadcast_to(owner_row, (fac_count, desks)), 1.0, 0.0)
    before = jnp.where(
        lax.broadcasted_iota(jnp.int32, (desks, desks), 0)
        < lax.broadcasted_iota(jnp.int32, (desks, desks), 1),
        1.0,
        0.0,
    )
    prefix = lax.dot_general(
        member.astype(jnp.bfloat16), before.astype(jnp.bfloat16), (((1,), (0,)), ((), ())),
        preferred_element_type=jnp.float32,
    )
    rank = jnp.sum(prefix * member, axis=0, keepdims=True).astype(jnp.int32)
    slot_row = owner_row * ROWS + rank
    placement = jnp.where(
        lax.broadcasted_iota(jnp.int32, (count, desks), 0)
        == jnp.broadcast_to(slot_row, (count, desks)),
        1.0,
        0.0,
    ).astype(jnp.bfloat16)
    placed = lax.dot_general(
        placement, sens_t[...], (((1,), (0,)), ((), ())), preferred_element_type=jnp.float32
    ).astype(jnp.bfloat16)
    masked = masked_rows(own[...], buckets[device])
    delta = lax.dot_general(
        placed, masked, (((1,), (1,)), ((), ())), preferred_element_type=jnp.float32
    )
    packed = delta[:, :LANES] + packed_tail(delta[:, LANES:])
    chunks = packed.reshape(fac_count, ROWS, LANES)
    out[...] = chunks
    coded[...] = encoded(chunks)
    copy.wait()


def gamma_kernel(
    meta, own, near, far, chip_near, chip_far, buckets, owner_row_ref, gamma, delta, coded, out, sums,
):
    del coded
    desks = owner_row_ref.shape[1]
    width = HORIZONS * own.shape[0]
    live = meta[0]
    sums[...] = jnp.zeros(sums.shape, jnp.float32)

    def pick(block, code):
        value = own[...]
        for index, ref in ((1, near), (2, far), (3, chip_near), (4, chip_far)):
            value = jnp.where(code == index, ref[...], value)
        return masked_rows(value, buckets[block])

    for slot in range(CAP):
        @pl.when(slot < live)
        def _(slot=slot):
            row_part = pick(meta[1 + 6 * slot], meta[2 + 6 * slot])
            col_part = pick(meta[3 + 6 * slot], meta[4 + 6 * slot])
            desk = meta[5 + 6 * slot]
            owner = meta[6 + 6 * slot]
            product = lax.dot_general(
                row_part, gamma[slot], (((1,), (0,)), ((), ())), preferred_element_type=jnp.float32
            )
            quad = 0.5 * jnp.sum(col_part.astype(jnp.float32) * product, axis=1, keepdims=True)
            diagonal = lax.broadcasted_iota(jnp.int32, (width, width), 0) == lax.broadcasted_iota(
                jnp.int32, (width, width), 1
            )
            quad_row = jnp.sum(
                jnp.where(diagonal, jnp.broadcast_to(quad, (width, width)), 0.0),
                axis=0,
                keepdims=True,
            )
            earlier = jnp.logical_and(
                owner_row_ref[...] == owner, lax.broadcasted_iota(jnp.int32, (1, desks), 1) < desk
            )
            rank = jnp.sum(jnp.where(earlier, 1.0, 0.0), axis=1, keepdims=True).astype(jnp.int32)
            rank = jnp.broadcast_to(rank, (ROWS, LANES))
            tail_row = jnp.concatenate([quad_row[:, LANES:]] * 4, axis=1)
            quarter = lax.broadcasted_iota(jnp.int32, (ROWS, LANES), 1) // 64
            row = lax.broadcasted_iota(jnp.int32, (ROWS, LANES), 0)
            moved = jnp.where(rank >= 4, 4, 0)
            in_tail = jnp.logical_and(
                row == DESK_DEV + jnp.where(rank >= 4, 1, 0), quarter == rank - moved
            )
            sums[slot] = jnp.where(
                row == rank,
                jnp.broadcast_to(quad_row[:, :LANES], (ROWS, LANES)),
                jnp.where(in_tail, jnp.broadcast_to(tail_row, (ROWS, LANES)), 0.0),
            )

    first = meta[6]
    second = jnp.where(live > 1, meta[12], first)
    joint = jnp.where(first == second, 1.0, 0.0)

    @pl.when(live > 0)
    def _():
        one = delta[first] + sums[0] + joint * sums[1]
        out[first] = encoded(one[None])[0]

    @pl.when(live > 1)
    def _():
        two = delta[second] + sums[1] + joint * sums[0]
        out[second] = encoded(two[None])[0]


def sum_kernel(received, packed, profit):
    lanes = 128
    value = received[...].astype(jnp.int32).astype(jnp.float32)
    value = value.reshape(received.shape[0] * 2, ROWS, lanes)
    scale = jnp.exp2(value[:, ROWS - 1 :, :])
    total = value * jnp.broadcast_to(scale, value.shape)
    total = jnp.sum(total.reshape(received.shape[0], 2, ROWS, lanes), axis=0)
    low, high = total[0], total[1]
    low_turned = pltpu.roll(low, 64, 1)
    high_turned = pltpu.roll(high, 64, 1)
    row = lax.broadcasted_iota(jnp.int32, (ROWS, lanes), 0)
    fifth = pltpu.roll(low, ROWS - DESK_DEV, 0)
    for j, source, shift in (
        (1, low_turned, 4), (2, high, 3), (3, high_turned, 2), (4, low, 2),
    ):
        moved = pltpu.roll(source, ROWS - shift, 0)
        fifth = jnp.where(row == j, moved, fifth)
    for h, block in enumerate((low, low_turned, high, high_turned, fifth)):
        packed[ROWS * h : ROWS * h + ROWS, :] = block
        for j in range(DESK_DEV):
            profit[j, h : h + 1, :] = block[j : j + 1, :64]


def tail_kernel(own, other1, other2, other3, shortfall, adjusted):
    lanes = 128
    count = HORIZONS * ROWS
    lane = lax.broadcasted_iota(jnp.int32, (count, lanes), 1)
    filler = jnp.zeros((lanes - count, lanes), jnp.float32)
    columns = []
    for one, two in ((own, other1), (other2, other3)):
        pair = -jnp.where(lane < 64, one[...], pltpu.roll(two[...], 64, 1))
        columns.append(jnp.transpose(jnp.concatenate([pair, filler], axis=0)))
    values = jnp.concatenate(columns, axis=0).reshape(32, 8, lanes)
    total = jnp.zeros((1, lanes), jnp.float32)
    left = jnp.full((1, lanes), float(TAIL), jnp.float32)
    for _ in range(TAIL):
        best = jnp.max(jnp.max(values, axis=0), axis=0, keepdims=True)
        same = values == jnp.broadcast_to(best[None], values.shape)
        found = jnp.sum(jnp.sum(jnp.where(same, 1.0, 0.0), axis=0), axis=0, keepdims=True)
        taken = jnp.minimum(found, left)
        total = total + jnp.where(taken > 0.0, taken * best, 0.0)
        left = left - taken
        values = jnp.where(same, -jnp.inf, values)
    mean = jnp.broadcast_to(total * (1.0 / TAIL), (ROWS, lanes))
    row = lax.broadcasted_iota(jnp.int32, (ROWS, lanes), 0)
    by_horizon = mean
    weight = jnp.full((ROWS, lanes), horizon_weights[0], jnp.float32)
    for h in range(1, HORIZONS):
        by_horizon = jnp.where(row == h, pltpu.roll(mean, lanes - ROWS * h, 1), by_horizon)
        weight = jnp.where(row == h, horizon_weights[h], weight)
    weight = jnp.where(row < HORIZONS, weight, 0.0)
    spent = jnp.sum(weight * by_horizon * by_horizon, axis=0, keepdims=True)
    adjusted[...] = jnp.sqrt(spent + 1e-06)[:, :DESK_DEV]
    square = jnp.concatenate([by_horizon, jnp.zeros((lanes - ROWS, lanes), jnp.float32)], axis=0)
    shortfall[...] = jnp.transpose(square)[:DESK_DEV, :HORIZONS]


VMEM = pl.BlockSpec(memory_space=pltpu.VMEM)
SMEM = pl.BlockSpec(memory_space=pltpu.SMEM)
HBM = pl.BlockSpec(memory_space=pltpu.HBM)
ORDER = (3, 1, 2, 0)
SCEN_ORDER = (2, 3, 1)


def held(value):
    return pltpu.with_memory_space_constraint(value, pltpu.VMEM)


def resident(value):
    return pltpu.with_memory_space_constraint(value, pltpu.HBM)


def limited(mib):
    return pltpu.CompilerParams(vmem_limit_bytes=mib << 20)


def local(
    loadings, reduced_shocks, sensitivity, cross_gamma, block_list, block_owner, desk_owner, buckets
):
    fac_count = lax.axis_size("fac")
    scen_count = lax.axis_size("scen")
    factors, s_dev = reduced_shocks.shape
    desks = desk_owner.shape[0]
    f32 = jnp.float32
    bf16 = jnp.bfloat16
    i32 = jnp.int32
    tile_shape = (fac_count, 8, BLK // 8)
    shocks, tiles, sens_t, owner_row, meta = pl.pallas_call(
        shocks_kernel,
        out_shape=(
            pltpu.VMEM((s_dev, BLK), bf16),
            pltpu.VMEM(tile_shape, i32),
            pltpu.VMEM((desks, BLK), bf16),
            pltpu.VMEM((1, desks), i32),
            pltpu.SMEM((16,), i32),
        ),
        in_specs=[HBM] * 8,
        out_specs=(VMEM, VMEM, VMEM, VMEM, SMEM),
        scratch_shapes=[
            pltpu.VMEM((factors, BLK), bf16),
            pltpu.VMEM((s_dev, factors), bf16),
            pltpu.SMEM(block_owner.shape, i32),
            pltpu.SMEM(block_list.shape[::-1], i32),
            pltpu.SMEM(desk_owner.shape, i32),
            pltpu.SemaphoreType.DMA((CHUNKS + 7,)),
        ],
        name="shocks",
        compiler_params=limited(10),
    )(
        *map(
            resident,
            (
                loadings.T, reduced_shocks.T, buckets.reshape(tile_shape), sensitivity.T,
                desk_owner.reshape(1, desks), block_owner, block_list.T, desk_owner,
            ),
        )
    )
    pairs = swap_pairs(fac_count)
    moved = {}
    for index in ORDER:
        moved[index] = held(lax.ppermute(shocks, "fac", pairs[index]))
    chunk_shape = (fac_count, ROWS, LANES)
    coded_shape = pltpu.VMEM((fac_count, 2 * ROWS, LANES // 2), jnp.int16)
    delta, coded, gamma = pl.pallas_call(
        delta_kernel,
        out_shape=(
            pltpu.VMEM(chunk_shape, f32), coded_shape, pltpu.VMEM(cross_gamma.shape, bf16)
        ),
        in_specs=[VMEM] * 4 + [HBM],
        out_specs=(VMEM, VMEM, VMEM),
        scratch_shapes=[pltpu.SemaphoreType.DMA],
        name="delta",
        compiler_params=limited(16),
    )(shocks, tiles, sens_t, owner_row, resident(cross_gamma))
    terms = pl.pallas_call(
        gamma_kernel,
        out_shape=coded_shape,
        in_specs=[SMEM] + [VMEM] * 10,
        out_specs=VMEM,
        scratch_shapes=[pltpu.VMEM((CAP, ROWS, LANES), f32)],
        input_output_aliases={10: 0},
        name="gamma",
        compiler_params=limited(16),
    )(meta, shocks, moved[0], moved[1], moved[2], moved[3], tiles, owner_row, gamma, delta, coded)
    received = held(lax.all_to_all(terms, "fac", 0, 0, tiled=False))
    packed, profit = pl.pallas_call(
        sum_kernel,
        out_shape=(
            pltpu.VMEM((HORIZONS * ROWS, 128), f32),
            jax.ShapeDtypeStruct((DESK_DEV, HORIZONS, s_dev), f32),
        ),
        in_specs=[VMEM],
        out_specs=(VMEM, VMEM),
        name="total",
        compiler_params=limited(8),
    )(received)
    others = []
    for step in SCEN_ORDER:
        others.append(held(lax.ppermute(packed, "scen", [(i, i ^ step) for i in range(scen_count)])))
    shortfall, adjusted = pl.pallas_call(
        tail_kernel,
        out_shape=(
            jax.ShapeDtypeStruct((DESK_DEV, HORIZONS), f32),
            jax.ShapeDtypeStruct((1, DESK_DEV), f32),
        ),
        in_specs=[VMEM] * scen_count,
        out_specs=(VMEM, VMEM),
        name="tail",
        compiler_params=limited(8),
    )(packed, *others)
    return (profit, shortfall, adjusted.reshape(DESK_DEV))


def solution(mesh):
    return jax.shard_map(
        local,
        mesh=mesh,
        in_specs=(
            P("fac", None),
            P(None, "scen"),
            P("fac", None),
            P("fac", None, None),
            P(),
            P(),
            P(),
            P(),
        ),
        out_specs=(P("fac", None, "scen"), P("fac", None), P("fac")),
        check_vma=False,
    )
```

```python
import jax
import jax.numpy as jnp
from jax import lax
from jax.experimental import pallas as pl
from jax.experimental.pallas import tpu as pltpu
from jax.sharding import PartitionSpec as P

BLK = 1024
HORIZONS = 5
CAP = 2
DESK_DEV = 5
ROWS = 8
LANES = 256
TAIL = 7
CHUNKS = 4

horizon_weights = (1.0, 1.0, 2.0, 2.0, 6.0)


def swap_pairs(count):
    near, chip_near, chip_far = [], [], []
    for index in range(count):
        near.append((index, index ^ 1))
        chip, core = divmod(index, 2)
        chip_near.append((index, (chip ^ 1) * 2 + core))
        other = ((chip + 1) ^ 1) - 1
        if 0 <= other < count // 2:
            chip_far.append((index, other * 2 + core))
    return near, chip_near, chip_far


def block_code(block, device):
    offset = block - device
    side = jnp.where(device % 2 == 0, offset, -offset)
    chip_side = jnp.where((device // 2) % 2 == 0, offset, -offset)
    beside = jnp.where(side > 0, 1, 2)
    apart = jnp.where(chip_side > 0, 3, 4)
    return jnp.where(offset == 0, 0, jnp.where(jnp.abs(offset) == 1, beside, apart))


def shocks_kernel(
    loadings_t, reduced_t, tiles_hbm, sens_hbm, owner_hbm, block_owner_hbm, block_list_hbm,
    desk_owner_hbm, shocks, tiles, sens_t, owner_row, meta, weights, factors, block_owner,
    block_list, desk_owner, sems,
):
    parts = CHUNKS
    span = BLK // parts
    copies = [pltpu.make_async_copy(reduced_t, factors, sems.at[parts])]
    for part in range(parts):
        window = pl.ds(part * span, span)
        copies.append(
            pltpu.make_async_copy(loadings_t.at[:, window], weights.at[:, window], sems.at[part])
        )
    scalars = [
        pltpu.make_async_copy(block_owner_hbm, block_owner, sems.at[parts + 1]),
        pltpu.make_async_copy(block_list_hbm, block_list, sems.at[parts + 2]),
        pltpu.make_async_copy(desk_owner_hbm, desk_owner, sems.at[parts + 3]),
    ]
    later = [
        pltpu.make_async_copy(owner_hbm, owner_row, sems.at[parts + 4]),
        pltpu.make_async_copy(tiles_hbm, tiles, sems.at[parts + 5]),
        pltpu.make_async_copy(sens_hbm, sens_t, sems.at[parts + 6]),
    ]
    for copy in scalars + copies + later:
        copy.start()
    for copy in scalars:
        copy.wait()
    device = lax.axis_index("fac")
    live = jnp.int32(0)
    first = jnp.int32(0)
    second = jnp.int32(0)
    for block in reversed(range(block_owner.shape[0])):
        hit = block_owner[block] == device
        second = jnp.where(hit, first, second)
        first = jnp.where(hit, block, first)
        live = live + jnp.where(hit, 1, 0)
    meta[0] = live
    for slot, block in enumerate((first, second)):
        row = block_list[0, block]
        col = block_list[1, block]
        desk = block_list[2, block]
        meta[1 + 6 * slot] = row
        meta[2 + 6 * slot] = block_code(row, device)
        meta[3 + 6 * slot] = col
        meta[4 + 6 * slot] = block_code(col, device)
        meta[5 + 6 * slot] = desk
        meta[6 + 6 * slot] = desk_owner[desk]
    copies[0].wait()
    for part in range(parts):
        copies[1 + part].wait()
        window = pl.ds(part * span, span)
        shocks[:, window] = lax.dot_general(
            factors[...], weights[:, window], (((1,), (0,)), ((), ())),
            preferred_element_type=jnp.float32,
        ).astype(jnp.bfloat16)
    for copy in later:
        copy.wait()


def lane_row(tile):
    return jnp.concatenate([tile[q : q + 1, :] for q in range(tile.shape[0])], axis=1)


def masked_rows(shocks, bucket_tile):
    bucket = jnp.broadcast_to(lane_row(bucket_tile), shocks.shape)
    value = shocks.astype(jnp.float32)
    pieces = [jnp.where(bucket >= h, value, 0.0) for h in range(HORIZONS)]
    return jnp.concatenate(pieces, axis=0).astype(jnp.bfloat16)


def packed_tail(tail):
    count = tail.shape[0]
    row = lax.broadcasted_iota(jnp.int32, (count, 64), 0) % ROWS
    pieces = []
    for q in range(4):
        piece = jnp.where(row == DESK_DEV, pltpu.roll(tail, DESK_DEV - q, 0), 0.0)
        if q == 0:
            piece = jnp.where(row == DESK_DEV + 1, pltpu.roll(tail, DESK_DEV - 3, 0), piece)
        pieces.append(piece)
    return jnp.concatenate(pieces, axis=1)


def encoded(chunks):
    largest = jnp.max(jnp.abs(chunks), axis=1, keepdims=True)
    exponent = jnp.ceil(jnp.log2(jnp.maximum(largest, 2.0**-100))) - 14.0
    shape = chunks.shape
    exponent = jnp.broadcast_to(exponent, shape)
    row = lax.broadcasted_iota(jnp.int32, shape, 1)
    value = jnp.where(row == ROWS - 1, exponent, jnp.round(chunks * jnp.exp2(-exponent)))
    value = jnp.concatenate([value[:, :, :128], value[:, :, 128:]], axis=1)
    return value.astype(jnp.int32).astype(jnp.int16)


def delta_kernel(own, buckets, sens_t, owner_row_ref, gamma_hbm, out, coded, gamma, sem):
    copy = pltpu.make_async_copy(gamma_hbm, gamma, sem)
    copy.start()
    desks = sens_t.shape[0]
    fac_count = out.shape[0]
    count = fac_count * ROWS
    device = lax.axis_index("fac")
    owner_row = owner_row_ref[...]
    groups = lax.broadcasted_iota(jnp.int32, (fac_count, desks), 0)
    member = jnp.where(groups == jnp.broadcast_to(owner_row, (fac_count, desks)), 1.0, 0.0)
    before = jnp.where(
        lax.broadcasted_iota(jnp.int32, (desks, desks), 0)
        < lax.broadcasted_iota(jnp.int32, (desks, desks), 1),
        1.0,
        0.0,
    )
    prefix = lax.dot_general(
        member.astype(jnp.bfloat16), before.astype(jnp.bfloat16), (((1,), (0,)), ((), ())),
        preferred_element_type=jnp.float32,
    )
    rank = jnp.sum(prefix * member, axis=0, keepdims=True).astype(jnp.int32)
    slot_row = owner_row * ROWS + rank
    placement = jnp.where(
        lax.broadcasted_iota(jnp.int32, (count, desks), 0)
        == jnp.broadcast_to(slot_row, (count, desks)),
        1.0,
        0.0,
    ).astype(jnp.bfloat16)
    placed = lax.dot_general(
        placement, sens_t[...], (((1,), (0,)), ((), ())), preferred_element_type=jnp.float32
    ).astype(jnp.bfloat16)
    masked = masked_rows(own[...], buckets[device])
    delta = lax.dot_general(
        placed, masked, (((1,), (1,)), ((), ())), preferred_element_type=jnp.float32
    )
    packed = delta[:, :LANES] + packed_tail(delta[:, LANES:])
    chunks = packed.reshape(fac_count, ROWS, LANES)
    out[...] = chunks
    coded[...] = encoded(chunks)
    copy.wait()


def gamma_kernel(
    meta, own, near, far, chip_near, chip_far, buckets, owner_row_ref, gamma, delta, coded, out, sums,
):
    del coded
    desks = owner_row_ref.shape[1]
    width = HORIZONS * own.shape[0]
    live = meta[0]
    sums[...] = jnp.zeros(sums.shape, jnp.float32)

    def pick(block, code):
        value = own[...]
        for index, ref in ((1, near), (2, far), (3, chip_near), (4, chip_far)):
            value = jnp.where(code == index, ref[...], value)
        return masked_rows(value, buckets[block])

    for slot in range(CAP):
        @pl.when(slot < live)
        def _(slot=slot):
            row_part = pick(meta[1 + 6 * slot], meta[2 + 6 * slot])
            col_part = pick(meta[3 + 6 * slot], meta[4 + 6 * slot])
            desk = meta[5 + 6 * slot]
            owner = meta[6 + 6 * slot]
            product = lax.dot_general(
                row_part, gamma[slot], (((1,), (0,)), ((), ())), preferred_element_type=jnp.float32
            )
            quad = 0.5 * jnp.sum(col_part.astype(jnp.float32) * product, axis=1, keepdims=True)
            diagonal = lax.broadcasted_iota(jnp.int32, (width, width), 0) == lax.broadcasted_iota(
                jnp.int32, (width, width), 1
            )
            quad_row = jnp.sum(
                jnp.where(diagonal, jnp.broadcast_to(quad, (width, width)), 0.0),
                axis=0,
                keepdims=True,
            )
            earlier = jnp.logical_and(
                owner_row_ref[...] == owner, lax.broadcasted_iota(jnp.int32, (1, desks), 1) < desk
            )
            rank = jnp.sum(jnp.where(earlier, 1.0, 0.0), axis=1, keepdims=True).astype(jnp.int32)
            rank = jnp.broadcast_to(rank, (ROWS, LANES))
            tail_row = jnp.concatenate([quad_row[:, LANES:]] * 4, axis=1)
            quarter = lax.broadcasted_iota(jnp.int32, (ROWS, LANES), 1) // 64
            row = lax.broadcasted_iota(jnp.int32, (ROWS, LANES), 0)
            moved = jnp.where(rank >= 4, 4, 0)
            in_tail = jnp.logical_and(
                row == DESK_DEV + jnp.where(rank >= 4, 1, 0), quarter == rank - moved
            )
            sums[slot] = jnp.where(
                row == rank,
                jnp.broadcast_to(quad_row[:, :LANES], (ROWS, LANES)),
                jnp.where(in_tail, jnp.broadcast_to(tail_row, (ROWS, LANES)), 0.0),
            )

    first = meta[6]
    second = jnp.where(live > 1, meta[12], first)
    joint = jnp.where(first == second, 1.0, 0.0)

    @pl.when(live > 0)
    def _():
        one = delta[first] + sums[0] + joint * sums[1]
        out[first] = encoded(one[None])[0]

    @pl.when(live > 1)
    def _():
        two = delta[second] + sums[1] + joint * sums[0]
        out[second] = encoded(two[None])[0]


def sum_kernel(received, packed, profit):
    lanes = 128
    value = received[...].astype(jnp.int32).astype(jnp.float32)
    value = value.reshape(received.shape[0] * 2, ROWS, lanes)
    scale = jnp.exp2(value[:, ROWS - 1 :, :])
    total = value * jnp.broadcast_to(scale, value.shape)
    total = jnp.sum(total.reshape(received.shape[0], 2, ROWS, lanes), axis=0)
    low, high = total[0], total[1]
    low_turned = pltpu.roll(low, 64, 1)
    high_turned = pltpu.roll(high, 64, 1)
    row = lax.broadcasted_iota(jnp.int32, (ROWS, lanes), 0)
    fifth = pltpu.roll(low, ROWS - DESK_DEV, 0)
    for j, source, shift in (
        (1, low_turned, 4), (2, high, 3), (3, high_turned, 2), (4, low, 2),
    ):
        moved = pltpu.roll(source, ROWS - shift, 0)
        fifth = jnp.where(row == j, moved, fifth)
    for h, block in enumerate((low, low_turned, high, high_turned, fifth)):
        packed[ROWS * h : ROWS * h + ROWS, :] = block
        for j in range(DESK_DEV):
            profit[j, h : h + 1, :] = block[j : j + 1, :64]


def tail_kernel(own, other1, other2, other3, shortfall, adjusted):
    lanes = 128
    count = HORIZONS * ROWS
    lane = lax.broadcasted_iota(jnp.int32, (count, lanes), 1)
    filler = jnp.zeros((lanes - count, lanes), jnp.float32)
    columns = []
    for one, two in ((own, other1), (other2, other3)):
        pair = -jnp.where(lane < 64, one[...], pltpu.roll(two[...], 64, 1))
        columns.append(jnp.transpose(jnp.concatenate([pair, filler], axis=0)))
    values = jnp.concatenate(columns, axis=0).reshape(32, 8, lanes)
    total = jnp.zeros((1, lanes), jnp.float32)
    left = jnp.full((1, lanes), float(TAIL), jnp.float32)
    for _ in range(TAIL):
        best = jnp.max(jnp.max(values, axis=0), axis=0, keepdims=True)
        same = values == jnp.broadcast_to(best[None], values.shape)
        found = jnp.sum(jnp.sum(jnp.where(same, 1.0, 0.0), axis=0), axis=0, keepdims=True)
        taken = jnp.minimum(found, left)
        total = total + jnp.where(taken > 0.0, taken * best, 0.0)
        left = left - taken
        values = jnp.where(same, -jnp.inf, values)
    mean = jnp.broadcast_to(total * (1.0 / TAIL), (ROWS, lanes))
    row = lax.broadcasted_iota(jnp.int32, (ROWS, lanes), 0)
    by_horizon = mean
    weight = jnp.full((ROWS, lanes), horizon_weights[0], jnp.float32)
    for h in range(1, HORIZONS):
        by_horizon = jnp.where(row == h, pltpu.roll(mean, lanes - ROWS * h, 1), by_horizon)
        weight = jnp.where(row == h, horizon_weights[h], weight)
    weight = jnp.where(row < HORIZONS, weight, 0.0)
    spent = jnp.sum(weight * by_horizon * by_horizon, axis=0, keepdims=True)
    adjusted[...] = jnp.sqrt(spent + 1e-06)[:, :DESK_DEV]
    square = jnp.concatenate([by_horizon, jnp.zeros((lanes - ROWS, lanes), jnp.float32)], axis=0)
    shortfall[...] = jnp.transpose(square)[:DESK_DEV, :HORIZONS]


VMEM = pl.BlockSpec(memory_space=pltpu.VMEM)
SMEM = pl.BlockSpec(memory_space=pltpu.SMEM)
HBM = pl.BlockSpec(memory_space=pltpu.HBM)
ORDER = (2, 1, 0)
SCEN_ORDER = (2, 3, 1)


def held(value):
    return pltpu.with_memory_space_constraint(value, pltpu.VMEM)


def resident(value):
    return pltpu.with_memory_space_constraint(value, pltpu.HBM)


def limited(mib):
    return pltpu.CompilerParams(vmem_limit_bytes=mib << 20)


def local(
    loadings, reduced_shocks, sensitivity, cross_gamma, block_list, block_owner, desk_owner, buckets
):
    fac_count = lax.axis_size("fac")
    scen_count = lax.axis_size("scen")
    factors, s_dev = reduced_shocks.shape
    desks = desk_owner.shape[0]
    f32 = jnp.float32
    bf16 = jnp.bfloat16
    i32 = jnp.int32
    tile_shape = (fac_count, 8, BLK // 8)
    shocks, tiles, sens_t, owner_row, meta = pl.pallas_call(
        shocks_kernel,
        out_shape=(
            pltpu.VMEM((s_dev, BLK), bf16),
            pltpu.VMEM(tile_shape, i32),
            pltpu.VMEM((desks, BLK), bf16),
            pltpu.VMEM((1, desks), i32),
            pltpu.SMEM((16,), i32),
        ),
        in_specs=[HBM] * 8,
        out_specs=(VMEM, VMEM, VMEM, VMEM, SMEM),
        scratch_shapes=[
            pltpu.VMEM((factors, BLK), bf16),
            pltpu.VMEM((s_dev, factors), bf16),
            pltpu.SMEM(block_owner.shape, i32),
            pltpu.SMEM(block_list.shape[::-1], i32),
            pltpu.SMEM(desk_owner.shape, i32),
            pltpu.SemaphoreType.DMA((CHUNKS + 7,)),
        ],
        name="shocks",
        compiler_params=limited(10),
    )(
        *map(
            resident,
            (
                loadings.T, reduced_shocks.T, buckets.reshape(tile_shape), sensitivity.T,
                desk_owner.reshape(1, desks), block_owner, block_list.T, desk_owner,
            ),
        )
    )
    pairs = swap_pairs(fac_count)
    moved = {}
    for index in ORDER:
        moved[index] = lax.ppermute(shocks, "fac", pairs[index])
    device = lax.axis_index("fac")
    onward = jnp.where((device % 2 == 0) == (device // 2 % 2 == 0), moved[1], moved[2])
    far = held(lax.ppermute(onward, "fac", pairs[0]))
    chunk_shape = (fac_count, ROWS, LANES)
    coded_shape = pltpu.VMEM((fac_count, 2 * ROWS, LANES // 2), jnp.int16)
    delta, coded, gamma = pl.pallas_call(
        delta_kernel,
        out_shape=(
            pltpu.VMEM(chunk_shape, f32), coded_shape, pltpu.VMEM(cross_gamma.shape, bf16)
        ),
        in_specs=[VMEM] * 4 + [HBM],
        out_specs=(VMEM, VMEM, VMEM),
        scratch_shapes=[pltpu.SemaphoreType.DMA],
        name="delta",
        compiler_params=limited(16),
    )(shocks, tiles, sens_t, owner_row, resident(cross_gamma))
    terms = pl.pallas_call(
        gamma_kernel,
        out_shape=coded_shape,
        in_specs=[SMEM] + [VMEM] * 10,
        out_specs=VMEM,
        scratch_shapes=[pltpu.VMEM((CAP, ROWS, LANES), f32)],
        input_output_aliases={10: 0},
        name="gamma",
        compiler_params=limited(16),
    )(meta, shocks, held(moved[0]), far, held(moved[1]), held(moved[2]), tiles, owner_row, gamma, delta, coded)
    received = held(lax.all_to_all(terms, "fac", 0, 0, tiled=False))
    packed, profit = pl.pallas_call(
        sum_kernel,
        out_shape=(
            pltpu.VMEM((HORIZONS * ROWS, 128), f32),
            jax.ShapeDtypeStruct((DESK_DEV, HORIZONS, s_dev), f32),
        ),
        in_specs=[VMEM],
        out_specs=(VMEM, VMEM),
        name="total",
        compiler_params=limited(8),
    )(received)
    others = []
    for step in SCEN_ORDER:
        others.append(held(lax.ppermute(packed, "scen", [(i, i ^ step) for i in range(scen_count)])))
    shortfall, adjusted = pl.pallas_call(
        tail_kernel,
        out_shape=(
            jax.ShapeDtypeStruct((DESK_DEV, HORIZONS), f32),
            jax.ShapeDtypeStruct((1, DESK_DEV), f32),
        ),
        in_specs=[VMEM] * scen_count,
        out_specs=(VMEM, VMEM),
        name="tail",
        compiler_params=limited(8),
    )(packed, *others)
    return (profit, shortfall, adjusted.reshape(DESK_DEV))


def solution(mesh):
    return jax.shard_map(
        local,
        mesh=mesh,
        in_specs=(
            P("fac", None),
            P(None, "scen"),
            P("fac", None),
            P("fac", None, None),
            P(),
            P(),
            P(),
            P(),
        ),
        out_specs=(P("fac", None, "scen"), P("fac", None), P("fac")),
        check_vma=False,
    )
```

```python
import jax
import jax.numpy as jnp
from jax import lax
from jax.experimental import pallas as pl
from jax.experimental.pallas import tpu as pltpu
from jax.sharding import PartitionSpec as P

BLK = 1024
HORIZONS = 5
CAP = 2
DESK_DEV = 5
ROWS = 8
LANES = 256
TAIL = 7
CHUNKS = 4
FAR = 2

horizon_weights = (1.0, 1.0, 2.0, 2.0, 6.0)


def swap_pairs(count):
    near, chip_near, chip_far = [], [], []
    for index in range(count):
        near.append((index, index ^ 1))
        chip, core = divmod(index, 2)
        chip_near.append((index, (chip ^ 1) * 2 + core))
        other = ((chip + 1) ^ 1) - 1
        if 0 <= other < count // 2:
            chip_far.append((index, other * 2 + core))
    return near, chip_near, chip_far


def block_code(block, device):
    offset = block - device
    side = jnp.where(device % 2 == 0, offset, -offset)
    chip_side = jnp.where((device // 2) % 2 == 0, offset, -offset)
    beside = jnp.where(side > 0, 1, 2)
    apart = jnp.where(chip_side > 0, 3, 4)
    return jnp.where(offset == 0, 0, jnp.where(jnp.abs(offset) == 1, beside, apart))


def shocks_kernel(
    loadings_t, reduced_t, tiles_hbm, owner_hbm, block_owner_hbm, block_list_hbm, desk_owner_hbm,
    shocks, tiles, owner_row, meta, weights, factors, block_owner, block_list, desk_owner, sems,
):
    parts = CHUNKS
    span = BLK // parts
    copies = [pltpu.make_async_copy(reduced_t, factors, sems.at[parts])]
    for part in range(parts):
        window = pl.ds(part * span, span)
        copies.append(
            pltpu.make_async_copy(loadings_t.at[:, window], weights.at[:, window], sems.at[part])
        )
    scalars = [
        pltpu.make_async_copy(block_owner_hbm, block_owner, sems.at[parts + 1]),
        pltpu.make_async_copy(block_list_hbm, block_list, sems.at[parts + 2]),
        pltpu.make_async_copy(desk_owner_hbm, desk_owner, sems.at[parts + 3]),
    ]
    later = [pltpu.make_async_copy(owner_hbm, owner_row, sems.at[parts + 4])]
    for copy in scalars + copies + later:
        copy.start()
    for copy in scalars:
        copy.wait()
    device = lax.axis_index("fac")
    live = jnp.int32(0)
    first = jnp.int32(0)
    second = jnp.int32(0)
    for block in reversed(range(block_owner.shape[0])):
        hit = block_owner[block] == device
        second = jnp.where(hit, first, second)
        first = jnp.where(hit, block, first)
        live = live + jnp.where(hit, 1, 0)
    meta[0] = live
    sources = [device]
    for slot, block in enumerate((first, second)):
        row = block_list[0, block]
        col = block_list[1, block]
        desk = block_list[2, block]
        meta[2 + 6 * slot] = block_code(row, device)
        meta[4 + 6 * slot] = block_code(col, device)
        meta[5 + 6 * slot] = desk
        meta[6 + 6 * slot] = desk_owner[desk]
        sources += [row, col]
    for index, block in enumerate(sources):
        copy = pltpu.make_async_copy(tiles_hbm.at[block], tiles.at[index], sems.at[parts + 5 + index])
        copy.start()
        later.append(copy)
    copies[0].wait()
    for part in range(parts):
        copies[1 + part].wait()
        window = pl.ds(part * span, span)
        shocks[:, window] = lax.dot_general(
            factors[...], weights[:, window], (((1,), (0,)), ((), ())),
            preferred_element_type=jnp.float32,
        ).astype(jnp.bfloat16)
    for copy in later:
        copy.wait()


def lane_row(tile):
    return jnp.concatenate([tile[q : q + 1, :] for q in range(tile.shape[0])], axis=1)


def masked_rows(shocks, bucket_tile):
    bucket = jnp.broadcast_to(lane_row(bucket_tile), shocks.shape)
    value = shocks.astype(jnp.float32)
    pieces = [jnp.where(bucket >= h, value, 0.0) for h in range(HORIZONS)]
    return jnp.concatenate(pieces, axis=0).astype(jnp.bfloat16)


def packed_tail(tail):
    count = tail.shape[0]
    row = lax.broadcasted_iota(jnp.int32, (count, 64), 0) % ROWS
    pieces = []
    for q in range(4):
        piece = jnp.where(row == DESK_DEV, pltpu.roll(tail, DESK_DEV - q, 0), 0.0)
        if q == 0:
            piece = jnp.where(row == DESK_DEV + 1, pltpu.roll(tail, DESK_DEV - 3, 0), piece)
        pieces.append(piece)
    return jnp.concatenate(pieces, axis=1)


def encoded(chunks):
    largest = jnp.max(jnp.abs(chunks), axis=1, keepdims=True)
    exponent = jnp.ceil(jnp.log2(jnp.maximum(largest, 2.0**-100))) - 14.0
    shape = chunks.shape
    exponent = jnp.broadcast_to(exponent, shape)
    row = lax.broadcasted_iota(jnp.int32, shape, 1)
    value = jnp.where(row == ROWS - 1, exponent, jnp.round(chunks * jnp.exp2(-exponent)))
    value = jnp.concatenate([value[:, :, :128], value[:, :, 128:]], axis=1)
    return value.astype(jnp.int32).astype(jnp.int16)


def delta_kernel(
    own, tiles, owner_row_ref, sens_hbm, gamma_hbm, out, coded, gamma, sens_t, sems
):
    sens_copy = pltpu.make_async_copy(sens_hbm, sens_t, sems.at[0])
    copy = pltpu.make_async_copy(gamma_hbm, gamma, sems.at[1])
    sens_copy.start()
    copy.start()
    desks = sens_t.shape[0]
    fac_count = out.shape[0]
    count = fac_count * ROWS
    owner_row = owner_row_ref[...]
    groups = lax.broadcasted_iota(jnp.int32, (fac_count, desks), 0)
    member = jnp.where(groups == jnp.broadcast_to(owner_row, (fac_count, desks)), 1.0, 0.0)
    before = jnp.where(
        lax.broadcasted_iota(jnp.int32, (desks, desks), 0)
        < lax.broadcasted_iota(jnp.int32, (desks, desks), 1),
        1.0,
        0.0,
    )
    prefix = lax.dot_general(
        member.astype(jnp.bfloat16), before.astype(jnp.bfloat16), (((1,), (0,)), ((), ())),
        preferred_element_type=jnp.float32,
    )
    rank = jnp.sum(prefix * member, axis=0, keepdims=True).astype(jnp.int32)
    slot_row = owner_row * ROWS + rank
    placement = jnp.where(
        lax.broadcasted_iota(jnp.int32, (count, desks), 0)
        == jnp.broadcast_to(slot_row, (count, desks)),
        1.0,
        0.0,
    ).astype(jnp.bfloat16)
    masked = masked_rows(own[...], tiles[0])
    sens_copy.wait()
    placed = lax.dot_general(
        placement, sens_t[...], (((1,), (0,)), ((), ())), preferred_element_type=jnp.float32
    ).astype(jnp.bfloat16)
    delta = lax.dot_general(
        placed, masked, (((1,), (1,)), ((), ())), preferred_element_type=jnp.float32
    )
    packed = delta[:, :LANES] + packed_tail(delta[:, LANES:])
    chunks = packed.reshape(fac_count, ROWS, LANES)
    out[...] = chunks
    coded[...] = encoded(chunks)
    copy.wait()


def picked(code, tile, own, others):
    value = own[...]
    for index, ref in others:
        value = jnp.where(code == index, ref[...], value)
    return masked_rows(value, tile)


def early_kernel(meta, own, near, chip_near, chip_far, tiles, gamma, product):
    others = ((1, near), (3, chip_near), (4, chip_far))
    for slot in range(CAP):
        row_code = meta[2 + 6 * slot]
        col_code = meta[4 + 6 * slot]
        live = slot < meta[0]

        @pl.when(jnp.logical_and(live, row_code != FAR))
        def _(slot=slot, row_code=row_code):
            part = picked(row_code, tiles[1 + 2 * slot], own, others)
            product[slot] = lax.dot_general(
                part, gamma[slot], (((1,), (0,)), ((), ())), preferred_element_type=jnp.float32
            )

        late = jnp.logical_and(row_code == FAR, col_code != FAR)

        @pl.when(jnp.logical_and(live, late))
        def _(slot=slot, col_code=col_code):
            part = picked(col_code, tiles[2 + 2 * slot], own, others)
            product[slot] = lax.dot_general(
                part, gamma[slot], (((1,), (1,)), ((), ())), preferred_element_type=jnp.float32
            )


def gamma_kernel(
    meta, own, near, far, chip_near, chip_far, tiles, owner_row_ref, gamma, product, delta, coded,
    out, sums, quads,
):
    del coded
    desks = owner_row_ref.shape[1]
    width = HORIZONS * own.shape[0]
    live = meta[0]
    sums[...] = jnp.zeros(sums.shape, jnp.float32)
    others = ((1, near), (FAR, far), (3, chip_near), (4, chip_far))

    for slot in range(CAP):
        @pl.when(slot < live)
        def _(slot=slot):
            row_code = meta[2 + 6 * slot]
            col_code = meta[4 + 6 * slot]
            desk = meta[5 + 6 * slot]
            owner = meta[6 + 6 * slot]
            use_row = row_code == FAR
            tile = jnp.where(use_row, tiles[1 + 2 * slot], tiles[2 + 2 * slot])
            part = picked(jnp.where(use_row, row_code, col_code), tile, own, others)
            whole = part.astype(jnp.float32)
            both = jnp.logical_and(use_row, col_code == FAR)

            @pl.when(both)
            def _():
                value = lax.dot_general(
                    part, gamma[slot], (((1,), (0,)), ((), ())), preferred_element_type=jnp.float32
                )
                quads[...] = jnp.sum(whole * value, axis=1, keepdims=True)

            @pl.when(jnp.logical_not(both))
            def _():
                quads[...] = jnp.sum(whole * product[slot], axis=1, keepdims=True)

            quad = 0.5 * quads[...]
            diagonal = lax.broadcasted_iota(jnp.int32, (width, width), 0) == lax.broadcasted_iota(
                jnp.int32, (width, width), 1
            )
            quad_row = jnp.sum(
                jnp.where(diagonal, jnp.broadcast_to(quad, (width, width)), 0.0),
                axis=0,
                keepdims=True,
            )
            earlier = jnp.logical_and(
                owner_row_ref[...] == owner, lax.broadcasted_iota(jnp.int32, (1, desks), 1) < desk
            )
            rank = jnp.sum(jnp.where(earlier, 1.0, 0.0), axis=1, keepdims=True).astype(jnp.int32)
            rank = jnp.broadcast_to(rank, (ROWS, LANES))
            tail_row = jnp.concatenate([quad_row[:, LANES:]] * 4, axis=1)
            quarter = lax.broadcasted_iota(jnp.int32, (ROWS, LANES), 1) // 64
            row = lax.broadcasted_iota(jnp.int32, (ROWS, LANES), 0)
            moved = jnp.where(rank >= 4, 4, 0)
            in_tail = jnp.logical_and(
                row == DESK_DEV + jnp.where(rank >= 4, 1, 0), quarter == rank - moved
            )
            sums[slot] = jnp.where(
                row == rank,
                jnp.broadcast_to(quad_row[:, :LANES], (ROWS, LANES)),
                jnp.where(in_tail, jnp.broadcast_to(tail_row, (ROWS, LANES)), 0.0),
            )

    first = meta[6]
    second = jnp.where(live > 1, meta[12], first)
    joint = jnp.where(first == second, 1.0, 0.0)

    @pl.when(live > 0)
    def _():
        one = delta[first] + sums[0] + joint * sums[1]
        out[first] = encoded(one[None])[0]

    @pl.when(live > 1)
    def _():
        two = delta[second] + sums[1] + joint * sums[0]
        out[second] = encoded(two[None])[0]


def sum_kernel(received, packed):
    lanes = 128
    value = received[...].astype(jnp.int32).astype(jnp.float32)
    value = value.reshape(received.shape[0] * 2, ROWS, lanes)
    scale = jnp.exp2(value[:, ROWS - 1 :, :])
    total = value * jnp.broadcast_to(scale, value.shape)
    total = jnp.sum(total.reshape(received.shape[0], 2, ROWS, lanes), axis=0)
    low, high = total[0], total[1]
    low_turned = pltpu.roll(low, 64, 1)
    high_turned = pltpu.roll(high, 64, 1)
    row = lax.broadcasted_iota(jnp.int32, (ROWS, lanes), 0)
    fifth = pltpu.roll(low, ROWS - DESK_DEV, 0)
    for j, source, shift in (
        (1, low_turned, 4), (2, high, 3), (3, high_turned, 2), (4, low, 2),
    ):
        moved = pltpu.roll(source, ROWS - shift, 0)
        fifth = jnp.where(row == j, moved, fifth)
    packed[...] = jnp.concatenate([low, high, fifth], axis=0)


def profit_kernel(packed, profit):
    for h in range(HORIZONS):
        start = 64 * (h % 2)
        block = packed[ROWS * (h // 2) : ROWS * (h // 2) + ROWS, start : start + 64]
        for j in range(DESK_DEV):
            profit[j, h : h + 1, :] = block[j : j + 1, :]


def tail_kernel(own, other1, other2, other3, shortfall, adjusted):
    lanes = 128
    count = HORIZONS * ROWS
    lower = lax.broadcasted_iota(jnp.int32, (3 * ROWS, lanes), 1) < 64
    filler = jnp.zeros((lanes - count, lanes), jnp.float32)
    columns = []
    for one, two in ((own, other1), (other2, other3)):
        even = jnp.where(lower, one[...], pltpu.roll(two[...], 64, 1))
        odd = jnp.where(lower, pltpu.roll(one[...], 64, 1), two[...])
        pair = -jnp.concatenate(
            [even[:ROWS], odd[:ROWS], even[ROWS : 2 * ROWS], odd[ROWS : 2 * ROWS], even[2 * ROWS :]],
            axis=0,
        )
        columns.append(jnp.transpose(jnp.concatenate([pair, filler], axis=0)))
    values = jnp.concatenate(columns, axis=0).reshape(32, 8, lanes)
    total = jnp.zeros((1, lanes), jnp.float32)
    left = jnp.full((1, lanes), float(TAIL), jnp.float32)
    for _ in range(TAIL):
        best = jnp.max(jnp.max(values, axis=0), axis=0, keepdims=True)
        same = values == jnp.broadcast_to(best[None], values.shape)
        found = jnp.sum(jnp.sum(jnp.where(same, 1.0, 0.0), axis=0), axis=0, keepdims=True)
        taken = jnp.minimum(found, left)
        total = total + jnp.where(taken > 0.0, taken * best, 0.0)
        left = left - taken
        values = jnp.where(same, -jnp.inf, values)
    mean = jnp.broadcast_to(total * (1.0 / TAIL), (ROWS, lanes))
    row = lax.broadcasted_iota(jnp.int32, (ROWS, lanes), 0)
    by_horizon = mean
    weight = jnp.full((ROWS, lanes), horizon_weights[0], jnp.float32)
    for h in range(1, HORIZONS):
        by_horizon = jnp.where(row == h, pltpu.roll(mean, lanes - ROWS * h, 1), by_horizon)
        weight = jnp.where(row == h, horizon_weights[h], weight)
    weight = jnp.where(row < HORIZONS, weight, 0.0)
    spent = jnp.sum(weight * by_horizon * by_horizon, axis=0, keepdims=True)
    adjusted[...] = jnp.sqrt(spent + 1e-06)[:, :DESK_DEV]
    square = jnp.concatenate([by_horizon, jnp.zeros((lanes - ROWS, lanes), jnp.float32)], axis=0)
    shortfall[...] = jnp.transpose(square)[:DESK_DEV, :HORIZONS]


VMEM = pl.BlockSpec(memory_space=pltpu.VMEM)
SMEM = pl.BlockSpec(memory_space=pltpu.SMEM)
HBM = pl.BlockSpec(memory_space=pltpu.HBM)
ORDER = (2, 1, 0)
SCEN_ORDER = (2, 3, 1)


def held(value):
    return pltpu.with_memory_space_constraint(value, pltpu.VMEM)


def resident(value):
    return pltpu.with_memory_space_constraint(value, pltpu.HBM)


def limited(mib):
    return pltpu.CompilerParams(vmem_limit_bytes=mib << 20)


def local(
    loadings, reduced_shocks, sensitivity, cross_gamma, block_list, block_owner, desk_owner, buckets
):
    fac_count = lax.axis_size("fac")
    scen_count = lax.axis_size("scen")
    factors, s_dev = reduced_shocks.shape
    desks = desk_owner.shape[0]
    f32 = jnp.float32
    bf16 = jnp.bfloat16
    i32 = jnp.int32
    tile_shape = (fac_count, 8, BLK // 8)
    shocks, tiles, owner_row, meta = pl.pallas_call(
        shocks_kernel,
        out_shape=(
            pltpu.VMEM((s_dev, BLK), bf16),
            pltpu.VMEM((1 + 2 * CAP, *tile_shape[1:]), i32),
            pltpu.VMEM((1, desks), i32),
            pltpu.SMEM((16,), i32),
        ),
        in_specs=[HBM] * 7,
        out_specs=(VMEM, VMEM, VMEM, SMEM),
        scratch_shapes=[
            pltpu.VMEM((factors, BLK), bf16),
            pltpu.VMEM((s_dev, factors), bf16),
            pltpu.SMEM(block_owner.shape, i32),
            pltpu.SMEM(block_list.shape[::-1], i32),
            pltpu.SMEM(desk_owner.shape, i32),
            pltpu.SemaphoreType.DMA((CHUNKS + 6 + 2 * CAP,)),
        ],
        name="shocks",
        compiler_params=limited(10),
    )(
        *map(
            resident,
            (
                loadings.T, reduced_shocks.T, buckets.reshape(tile_shape),
                desk_owner.reshape(1, desks), block_owner, block_list.T, desk_owner,
            ),
        )
    )
    pairs = swap_pairs(fac_count)
    moved = {}
    for index in ORDER:
        moved[index] = lax.ppermute(shocks, "fac", pairs[index])
    chunk_shape = (fac_count, ROWS, LANES)
    coded_shape = pltpu.VMEM((fac_count, 2 * ROWS, LANES // 2), jnp.int16)
    delta, coded, gamma = pl.pallas_call(
        delta_kernel,
        out_shape=(
            pltpu.VMEM(chunk_shape, f32), coded_shape, pltpu.VMEM(cross_gamma.shape, bf16)
        ),
        in_specs=[VMEM] * 3 + [HBM] * 2,
        out_specs=(VMEM, VMEM, VMEM),
        scratch_shapes=[pltpu.VMEM((desks, BLK), bf16), pltpu.SemaphoreType.DMA((2,))],
        name="delta",
        compiler_params=limited(16),
    )(shocks, tiles, owner_row, resident(sensitivity.T), resident(cross_gamma))
    device = lax.axis_index("fac")
    onward = jnp.where((device % 2 == 0) == (device // 2 % 2 == 0), moved[1], moved[2])
    far = held(lax.ppermute(onward, "fac", pairs[0]))
    nearby, chip_near, chip_far = (held(moved[index]) for index in range(3))
    product = pl.pallas_call(
        early_kernel,
        out_shape=pltpu.VMEM((CAP, HORIZONS * s_dev, BLK), f32),
        in_specs=[SMEM] + [VMEM] * 6,
        out_specs=VMEM,
        name="early",
        compiler_params=limited(12),
    )(meta, shocks, nearby, chip_near, chip_far, tiles, gamma)
    terms = pl.pallas_call(
        gamma_kernel,
        out_shape=coded_shape,
        in_specs=[SMEM] + [VMEM] * 11,
        out_specs=VMEM,
        scratch_shapes=[
            pltpu.VMEM((CAP, ROWS, LANES), f32),
            pltpu.VMEM((HORIZONS * s_dev, 1), f32),
        ],
        input_output_aliases={11: 0},
        name="gamma",
        compiler_params=limited(16),
    )(
        meta, shocks, nearby, far, chip_near, chip_far, tiles, owner_row, gamma, product, delta,
        coded,
    )
    received = held(lax.all_to_all(terms, "fac", 0, 0, tiled=False))
    packed = pl.pallas_call(
        sum_kernel,
        out_shape=pltpu.VMEM((3 * ROWS, 128), f32),
        in_specs=[VMEM],
        out_specs=VMEM,
        name="total",
        compiler_params=limited(8),
    )(received)
    profit = pl.pallas_call(
        profit_kernel,
        out_shape=jax.ShapeDtypeStruct((DESK_DEV, HORIZONS, s_dev), f32),
        in_specs=[VMEM],
        out_specs=VMEM,
        name="profit",
        compiler_params=limited(4),
    )(packed)
    others = []
    for step in SCEN_ORDER:
        others.append(held(lax.ppermute(packed, "scen", [(i, i ^ step) for i in range(scen_count)])))
    shortfall, adjusted = pl.pallas_call(
        tail_kernel,
        out_shape=(
            jax.ShapeDtypeStruct((DESK_DEV, HORIZONS), f32),
            jax.ShapeDtypeStruct((1, DESK_DEV), f32),
        ),
        in_specs=[VMEM] * scen_count,
        out_specs=(VMEM, VMEM),
        name="tail",
        compiler_params=limited(8),
    )(packed, *others)
    return (profit, shortfall, adjusted.reshape(DESK_DEV))


def solution(mesh):
    return jax.shard_map(
        local,
        mesh=mesh,
        in_specs=(
            P("fac", None),
            P(None, "scen"),
            P("fac", None),
            P("fac", None, None),
            P(),
            P(),
            P(),
            P(),
        ),
        out_specs=(P("fac", None, "scen"), P("fac", None), P("fac")),
        check_vma=False,
    )
```

```python
import jax
import jax.numpy as jnp
from jax import lax
from jax.experimental import pallas as pl
from jax.experimental.pallas import tpu as pltpu
from jax.sharding import PartitionSpec as P

BLK = 1024
HORIZONS = 5
CAP = 2
DESK_DEV = 5
ROWS = 8
LANES = 256
TAIL = 7
CHUNKS = 2
FAR = 2

horizon_weights = (1.0, 1.0, 2.0, 2.0, 6.0)


def swap_pairs(count):
    near, chip_near, chip_far = [], [], []
    for index in range(count):
        near.append((index, index ^ 1))
        chip, core = divmod(index, 2)
        chip_near.append((index, (chip ^ 1) * 2 + core))
        other = ((chip + 1) ^ 1) - 1
        if 0 <= other < count // 2:
            chip_far.append((index, other * 2 + core))
    return near, chip_near, chip_far


def block_code(block, device):
    offset = block - device
    side = jnp.where(device % 2 == 0, offset, -offset)
    chip_side = jnp.where((device // 2) % 2 == 0, offset, -offset)
    beside = jnp.where(side > 0, 1, 2)
    apart = jnp.where(chip_side > 0, 3, 4)
    return jnp.where(offset == 0, 0, jnp.where(jnp.abs(offset) == 1, beside, apart))


def shocks_kernel(
    loadings_t, reduced_t, tiles_hbm, owner_hbm, block_owner_hbm, block_list_hbm, desk_owner_hbm,
    shocks, tiles, owner_row, meta, weights, factors, block_owner, block_list, desk_owner, sems,
):
    parts = CHUNKS
    span = BLK // parts
    copies = [pltpu.make_async_copy(reduced_t, factors, sems.at[parts])]
    for part in range(parts):
        window = pl.ds(part * span, span)
        copies.append(
            pltpu.make_async_copy(loadings_t.at[:, window], weights.at[:, window], sems.at[part])
        )
    scalars = [
        pltpu.make_async_copy(block_owner_hbm, block_owner, sems.at[parts + 1]),
        pltpu.make_async_copy(block_list_hbm, block_list, sems.at[parts + 2]),
        pltpu.make_async_copy(desk_owner_hbm, desk_owner, sems.at[parts + 3]),
    ]
    later = [pltpu.make_async_copy(owner_hbm, owner_row, sems.at[parts + 4])]
    for copy in scalars + copies + later:
        copy.start()
    for copy in scalars:
        copy.wait()
    device = lax.axis_index("fac")
    live = jnp.int32(0)
    first = jnp.int32(0)
    second = jnp.int32(0)
    for block in reversed(range(block_owner.shape[0])):
        hit = block_owner[block] == device
        second = jnp.where(hit, first, second)
        first = jnp.where(hit, block, first)
        live = live + jnp.where(hit, 1, 0)
    meta[0] = live
    sources = [device]
    for slot, block in enumerate((first, second)):
        row = block_list[0, block]
        col = block_list[1, block]
        desk = block_list[2, block]
        meta[2 + 6 * slot] = block_code(row, device)
        meta[4 + 6 * slot] = block_code(col, device)
        meta[5 + 6 * slot] = desk
        meta[6 + 6 * slot] = desk_owner[desk]
        sources += [row, col]
    for index, block in enumerate(sources):
        copy = pltpu.make_async_copy(tiles_hbm.at[block], tiles.at[index], sems.at[parts + 5 + index])
        copy.start()
        later.append(copy)
    copies[0].wait()
    for part in range(parts):
        copies[1 + part].wait()
        window = pl.ds(part * span, span)
        shocks[:, window] = lax.dot_general(
            factors[...], weights[:, window], (((1,), (0,)), ((), ())),
            preferred_element_type=jnp.float32,
        ).astype(jnp.bfloat16)
    for copy in later:
        copy.wait()


def lane_row(tile):
    return jnp.concatenate([tile[q : q + 1, :] for q in range(tile.shape[0])], axis=1)


def masked_rows(shocks, bucket_tile):
    bucket = jnp.broadcast_to(lane_row(bucket_tile), shocks.shape)
    value = shocks.astype(jnp.float32)
    pieces = [jnp.where(bucket >= h, value, 0.0) for h in range(HORIZONS)]
    return jnp.concatenate(pieces, axis=0).astype(jnp.bfloat16)


def packed_tail(tail):
    count = tail.shape[0]
    row = lax.broadcasted_iota(jnp.int32, (count, 64), 0) % ROWS
    pieces = []
    for q in range(4):
        piece = jnp.where(row == DESK_DEV, pltpu.roll(tail, DESK_DEV - q, 0), 0.0)
        if q == 0:
            piece = jnp.where(row == DESK_DEV + 1, pltpu.roll(tail, DESK_DEV - 3, 0), piece)
        pieces.append(piece)
    return jnp.concatenate(pieces, axis=1)


def encoded(chunks):
    largest = jnp.max(jnp.abs(chunks), axis=1, keepdims=True)
    exponent = jnp.ceil(jnp.log2(jnp.maximum(largest, 2.0**-100))) - 14.0
    shape = chunks.shape
    exponent = jnp.broadcast_to(exponent, shape)
    row = lax.broadcasted_iota(jnp.int32, shape, 1)
    value = jnp.where(row == ROWS - 1, exponent, jnp.round(chunks * jnp.exp2(-exponent)))
    value = jnp.concatenate([value[:, :, :128], value[:, :, 128:]], axis=1)
    return value.astype(jnp.int32).astype(jnp.int16)


def delta_kernel(
    meta, own, tiles, owner_row_ref, sens_hbm, gamma_hbm, out, coded, gamma, ranks, sens_t, sems
):
    sens_copy = pltpu.make_async_copy(sens_hbm, sens_t, sems.at[0])
    copy = pltpu.make_async_copy(gamma_hbm, gamma, sems.at[1])
    sens_copy.start()
    copy.start()
    desks = sens_t.shape[0]
    fac_count = out.shape[0]
    count = fac_count * ROWS
    owner_row = owner_row_ref[...]
    groups = lax.broadcasted_iota(jnp.int32, (fac_count, desks), 0)
    member = jnp.where(groups == jnp.broadcast_to(owner_row, (fac_count, desks)), 1.0, 0.0)
    before = jnp.where(
        lax.broadcasted_iota(jnp.int32, (desks, desks), 0)
        < lax.broadcasted_iota(jnp.int32, (desks, desks), 1),
        1.0,
        0.0,
    )
    prefix = lax.dot_general(
        member.astype(jnp.bfloat16), before.astype(jnp.bfloat16), (((1,), (0,)), ((), ())),
        preferred_element_type=jnp.float32,
    )
    rank = jnp.sum(prefix * member, axis=0, keepdims=True).astype(jnp.int32)
    slot_row = owner_row * ROWS + rank
    placement = jnp.where(
        lax.broadcasted_iota(jnp.int32, (count, desks), 0)
        == jnp.broadcast_to(slot_row, (count, desks)),
        1.0,
        0.0,
    ).astype(jnp.bfloat16)
    masked = masked_rows(own[...], tiles[0])
    sens_copy.wait()
    placed = lax.dot_general(
        placement, sens_t[...], (((1,), (0,)), ((), ())), preferred_element_type=jnp.float32
    ).astype(jnp.bfloat16)
    delta = lax.dot_general(
        placed, masked, (((1,), (1,)), ((), ())), preferred_element_type=jnp.float32
    )
    packed = delta[:, :LANES] + packed_tail(delta[:, LANES:])
    chunks = packed.reshape(fac_count, ROWS, LANES)
    out[...] = chunks
    coded[...] = encoded(chunks)
    for slot in range(CAP):
        earlier = jnp.logical_and(
            owner_row == meta[6 + 6 * slot],
            lax.broadcasted_iota(jnp.int32, (1, desks), 1) < meta[5 + 6 * slot],
        )
        found = jnp.sum(jnp.where(earlier, 1.0, 0.0), axis=1, keepdims=True).astype(jnp.int32)
        ranks[slot] = jnp.broadcast_to(found, (ROWS, 128))
    copy.wait()


def picked(code, tile, own, others):
    value = own[...]
    for index, ref in others:
        value = jnp.where(code == index, ref[...], value)
    return masked_rows(value, tile)


def early_kernel(meta, own, near, chip_near, chip_far, tiles, gamma, product):
    others = ((1, near), (3, chip_near), (4, chip_far))
    for slot in range(CAP):
        row_code = meta[2 + 6 * slot]
        col_code = meta[4 + 6 * slot]
        live = slot < meta[0]

        @pl.when(jnp.logical_and(live, row_code != FAR))
        def _(slot=slot, row_code=row_code):
            part = picked(row_code, tiles[1 + 2 * slot], own, others)
            product[slot] = lax.dot_general(
                part, gamma[slot], (((1,), (0,)), ((), ())), preferred_element_type=jnp.float32
            )

        late = jnp.logical_and(row_code == FAR, col_code != FAR)

        @pl.when(jnp.logical_and(live, late))
        def _(slot=slot, col_code=col_code):
            part = picked(col_code, tiles[2 + 2 * slot], own, others)
            product[slot] = lax.dot_general(
                part, gamma[slot], (((1,), (1,)), ((), ())), preferred_element_type=jnp.float32
            )


def gamma_kernel(
    meta, own, near, far, chip_near, chip_far, tiles, ranks, gamma, early, delta, coded,
    out, product,
):
    del coded, early
    width = HORIZONS * own.shape[0]
    live = meta[0]
    others = ((1, near), (FAR, far), (3, chip_near), (4, chip_far))
    for slot in range(CAP):
        both = jnp.logical_and(meta[2 + 6 * slot] == FAR, meta[4 + 6 * slot] == FAR)

        @pl.when(jnp.logical_and(slot < live, both))
        def _(slot=slot):
            part = masked_rows(far[...], tiles[1 + 2 * slot])
            product[slot] = lax.dot_general(
                part, gamma[slot], (((1,), (0,)), ((), ())), preferred_element_type=jnp.float32
            )

    diagonal = lax.broadcasted_iota(jnp.int32, (width, width), 0) == lax.broadcasted_iota(
        jnp.int32, (width, width), 1
    )
    quarter = lax.broadcasted_iota(jnp.int32, (ROWS, LANES), 1) // 64
    row = lax.broadcasted_iota(jnp.int32, (ROWS, LANES), 0)
    sums = []
    for slot in range(CAP):
        row_code = meta[2 + 6 * slot]
        use_row = row_code == FAR
        tile = jnp.where(use_row, tiles[1 + 2 * slot], tiles[2 + 2 * slot])
        part = picked(jnp.where(use_row, row_code, meta[4 + 6 * slot]), tile, own, others)
        quad = 0.5 * jnp.sum(part.astype(jnp.float32) * product[slot], axis=1, keepdims=True)
        quad_row = jnp.sum(
            jnp.where(diagonal, jnp.broadcast_to(quad, (width, width)), 0.0), axis=0, keepdims=True
        )
        rank = jnp.concatenate([ranks[slot]] * 2, axis=1)
        tail_row = jnp.concatenate([quad_row[:, LANES:]] * 4, axis=1)
        moved = jnp.where(rank >= 4, 4, 0)
        in_tail = jnp.logical_and(
            row == DESK_DEV + jnp.where(rank >= 4, 1, 0), quarter == rank - moved
        )
        addend = jnp.where(
            row == rank,
            jnp.broadcast_to(quad_row[:, :LANES], (ROWS, LANES)),
            jnp.where(in_tail, jnp.broadcast_to(tail_row, (ROWS, LANES)), 0.0),
        )
        sums.append(jnp.where(slot < live, addend, 0.0))
    first = meta[6]
    second = jnp.where(live > 1, meta[12], first)
    same = first == second
    one = delta[first] + sums[0] + jnp.where(same, sums[1], 0.0)
    two = delta[second] + sums[1] + jnp.where(same, sums[0], 0.0)
    out[first] = encoded(one[None])[0]
    out[second] = encoded(two[None])[0]


def sum_kernel(received, packed):
    lanes = 128
    value = received[...].astype(jnp.int32).astype(jnp.float32)
    value = value.reshape(received.shape[0] * 2, ROWS, lanes)
    scale = jnp.exp2(value[:, ROWS - 1 :, :])
    total = value * jnp.broadcast_to(scale, value.shape)
    total = jnp.sum(total.reshape(received.shape[0], 2, ROWS, lanes), axis=0)
    low, high = total[0], total[1]
    low_turned = pltpu.roll(low, 64, 1)
    high_turned = pltpu.roll(high, 64, 1)
    row = lax.broadcasted_iota(jnp.int32, (ROWS, lanes), 0)
    fifth = pltpu.roll(low, ROWS - DESK_DEV, 0)
    for j, source, shift in (
        (1, low_turned, 4), (2, high, 3), (3, high_turned, 2), (4, low, 2),
    ):
        moved = pltpu.roll(source, ROWS - shift, 0)
        fifth = jnp.where(row == j, moved, fifth)
    packed[...] = jnp.concatenate([low, high, fifth], axis=0)


def profit_kernel(packed, profit):
    for h in range(HORIZONS):
        start = 64 * (h % 2)
        block = packed[ROWS * (h // 2) : ROWS * (h // 2) + ROWS, start : start + 64]
        for j in range(DESK_DEV):
            profit[j, h : h + 1, :] = block[j : j + 1, :]


def tail_kernel(own, other1, other2, other3, shortfall, adjusted):
    lanes = 128
    count = HORIZONS * ROWS
    lower = lax.broadcasted_iota(jnp.int32, (3 * ROWS, lanes), 1) < 64
    filler = jnp.zeros((lanes - count, lanes), jnp.float32)
    columns = []
    for one, two in ((own, other1), (other2, other3)):
        even = jnp.where(lower, one[...], pltpu.roll(two[...], 64, 1))
        odd = jnp.where(lower, pltpu.roll(one[...], 64, 1), two[...])
        pair = -jnp.concatenate(
            [even[:ROWS], odd[:ROWS], even[ROWS : 2 * ROWS], odd[ROWS : 2 * ROWS], even[2 * ROWS :]],
            axis=0,
        )
        columns.append(jnp.transpose(jnp.concatenate([pair, filler], axis=0)))
    values = jnp.concatenate(columns, axis=0).reshape(32, 8, lanes)
    total = jnp.zeros((1, lanes), jnp.float32)
    left = jnp.full((1, lanes), float(TAIL), jnp.float32)
    for _ in range(TAIL):
        best = jnp.max(jnp.max(values, axis=0), axis=0, keepdims=True)
        same = values == jnp.broadcast_to(best[None], values.shape)
        found = jnp.sum(jnp.sum(jnp.where(same, 1.0, 0.0), axis=0), axis=0, keepdims=True)
        taken = jnp.minimum(found, left)
        total = total + jnp.where(taken > 0.0, taken * best, 0.0)
        left = left - taken
        values = jnp.where(same, -jnp.inf, values)
    mean = jnp.broadcast_to(total * (1.0 / TAIL), (ROWS, lanes))
    row = lax.broadcasted_iota(jnp.int32, (ROWS, lanes), 0)
    by_horizon = mean
    weight = jnp.full((ROWS, lanes), horizon_weights[0], jnp.float32)
    for h in range(1, HORIZONS):
        by_horizon = jnp.where(row == h, pltpu.roll(mean, lanes - ROWS * h, 1), by_horizon)
        weight = jnp.where(row == h, horizon_weights[h], weight)
    weight = jnp.where(row < HORIZONS, weight, 0.0)
    spent = jnp.sum(weight * by_horizon * by_horizon, axis=0, keepdims=True)
    adjusted[...] = jnp.sqrt(spent + 1e-06)[:, :DESK_DEV]
    square = jnp.concatenate([by_horizon, jnp.zeros((lanes - ROWS, lanes), jnp.float32)], axis=0)
    shortfall[...] = jnp.transpose(square)[:DESK_DEV, :HORIZONS]


VMEM = pl.BlockSpec(memory_space=pltpu.VMEM)
SMEM = pl.BlockSpec(memory_space=pltpu.SMEM)
HBM = pl.BlockSpec(memory_space=pltpu.HBM)
ORDER = (2, 1, 0)
SCEN_ORDER = (2, 3, 1)


def held(value):
    return pltpu.with_memory_space_constraint(value, pltpu.VMEM)


def resident(value):
    return pltpu.with_memory_space_constraint(value, pltpu.HBM)


def limited(mib):
    return pltpu.CompilerParams(vmem_limit_bytes=mib << 20)


def local(
    loadings, reduced_shocks, sensitivity, cross_gamma, block_list, block_owner, desk_owner, buckets
):
    fac_count = lax.axis_size("fac")
    scen_count = lax.axis_size("scen")
    factors, s_dev = reduced_shocks.shape
    desks = desk_owner.shape[0]
    f32 = jnp.float32
    bf16 = jnp.bfloat16
    i32 = jnp.int32
    tile_shape = (fac_count, 8, BLK // 8)
    shocks, tiles, owner_row, meta = pl.pallas_call(
        shocks_kernel,
        out_shape=(
            pltpu.VMEM((s_dev, BLK), bf16),
            pltpu.VMEM((1 + 2 * CAP, *tile_shape[1:]), i32),
            pltpu.VMEM((1, desks), i32),
            pltpu.SMEM((16,), i32),
        ),
        in_specs=[HBM] * 7,
        out_specs=(VMEM, VMEM, VMEM, SMEM),
        scratch_shapes=[
            pltpu.VMEM((factors, BLK), bf16),
            pltpu.VMEM((s_dev, factors), bf16),
            pltpu.SMEM(block_owner.shape, i32),
            pltpu.SMEM(block_list.shape[::-1], i32),
            pltpu.SMEM(desk_owner.shape, i32),
            pltpu.SemaphoreType.DMA((CHUNKS + 6 + 2 * CAP,)),
        ],
        name="shocks",
        compiler_params=limited(10),
    )(
        *map(
            resident,
            (
                loadings.T, reduced_shocks.T, buckets.reshape(tile_shape),
                desk_owner.reshape(1, desks), block_owner, block_list.T, desk_owner,
            ),
        )
    )
    pairs = swap_pairs(fac_count)
    moved = {}
    for index in ORDER:
        moved[index] = lax.ppermute(shocks, "fac", pairs[index])
    chunk_shape = (fac_count, ROWS, LANES)
    coded_shape = pltpu.VMEM((fac_count, 2 * ROWS, LANES // 2), jnp.int16)
    delta, coded, gamma, ranks = pl.pallas_call(
        delta_kernel,
        out_shape=(
            pltpu.VMEM(chunk_shape, f32), coded_shape, pltpu.VMEM(cross_gamma.shape, bf16),
            pltpu.VMEM((CAP, ROWS, 128), i32),
        ),
        in_specs=[SMEM] + [VMEM] * 3 + [HBM] * 2,
        out_specs=(VMEM, VMEM, VMEM, VMEM),
        scratch_shapes=[pltpu.VMEM((desks, BLK), bf16), pltpu.SemaphoreType.DMA((2,))],
        name="delta",
        compiler_params=limited(16),
    )(meta, shocks, tiles, owner_row, resident(sensitivity.T), resident(cross_gamma))
    device = lax.axis_index("fac")
    onward = jnp.where((device % 2 == 0) == (device // 2 % 2 == 0), moved[1], moved[2])
    far = held(lax.ppermute(onward, "fac", pairs[0]))
    nearby, chip_near, chip_far = (held(moved[index]) for index in range(3))
    product_shape = pltpu.VMEM((CAP, HORIZONS * s_dev, BLK), f32)
    product = pl.pallas_call(
        early_kernel,
        out_shape=product_shape,
        in_specs=[SMEM] + [VMEM] * 6,
        out_specs=VMEM,
        name="early",
        compiler_params=limited(12),
    )(meta, shocks, nearby, chip_near, chip_far, tiles, gamma)
    terms, _ = pl.pallas_call(
        gamma_kernel,
        out_shape=(coded_shape, product_shape),
        in_specs=[SMEM] + [VMEM] * 11,
        out_specs=(VMEM, VMEM),
        input_output_aliases={11: 0, 9: 1},
        name="gamma",
        compiler_params=limited(16),
    )(
        meta, shocks, nearby, far, chip_near, chip_far, tiles, ranks, gamma, product, delta,
        coded,
    )
    received = held(lax.all_to_all(terms, "fac", 0, 0, tiled=False))
    packed = pl.pallas_call(
        sum_kernel,
        out_shape=pltpu.VMEM((3 * ROWS, 128), f32),
        in_specs=[VMEM],
        out_specs=VMEM,
        name="total",
        compiler_params=limited(8),
    )(received)
    profit = pl.pallas_call(
        profit_kernel,
        out_shape=jax.ShapeDtypeStruct((DESK_DEV, HORIZONS, s_dev), f32),
        in_specs=[VMEM],
        out_specs=VMEM,
        name="profit",
        compiler_params=limited(4),
    )(packed)
    others = []
    for step in SCEN_ORDER:
        others.append(held(lax.ppermute(packed, "scen", [(i, i ^ step) for i in range(scen_count)])))
    shortfall, adjusted = pl.pallas_call(
        tail_kernel,
        out_shape=(
            jax.ShapeDtypeStruct((DESK_DEV, HORIZONS), f32),
            jax.ShapeDtypeStruct((1, DESK_DEV), f32),
        ),
        in_specs=[VMEM] * scen_count,
        out_specs=(VMEM, VMEM),
        name="tail",
        compiler_params=limited(8),
    )(packed, *others)
    return (profit, shortfall, adjusted.reshape(DESK_DEV))


def solution(mesh):
    return jax.shard_map(
        local,
        mesh=mesh,
        in_specs=(
            P("fac", None),
            P(None, "scen"),
            P("fac", None),
            P("fac", None, None),
            P(),
            P(),
            P(),
            P(),
        ),
        out_specs=(P("fac", None, "scen"), P("fac", None), P("fac")),
        check_vma=False,
    )
```

```python
import jax
import jax.numpy as jnp
from jax import lax
from jax.experimental import pallas as pl
from jax.experimental.pallas import tpu as pltpu
from jax.sharding import PartitionSpec as P

BLK = 1024
HORIZONS = 5
CAP = 2
DESK_DEV = 5
ROWS = 8
LANES = 256
TAIL = 7
CHUNKS = 2
FAR = 2

horizon_weights = (1.0, 1.0, 2.0, 2.0, 6.0)


def swap_pairs(count):
    near, chip_near, chip_far = [], [], []
    for index in range(count):
        near.append((index, index ^ 1))
        chip, core = divmod(index, 2)
        chip_near.append((index, (chip ^ 1) * 2 + core))
        other = ((chip + 1) ^ 1) - 1
        if 0 <= other < count // 2:
            chip_far.append((index, other * 2 + core))
    return near, chip_near, chip_far


def block_code(block, device):
    offset = block - device
    side = jnp.where(device % 2 == 0, offset, -offset)
    chip_side = jnp.where((device // 2) % 2 == 0, offset, -offset)
    beside = jnp.where(side > 0, 1, 2)
    apart = jnp.where(chip_side > 0, 3, 4)
    return jnp.where(offset == 0, 0, jnp.where(jnp.abs(offset) == 1, beside, apart))


def shocks_kernel(
    loadings_t, reduced_t, tiles_hbm, owner_hbm, block_owner_hbm, block_list_hbm, desk_owner_hbm,
    shocks, tiles, owner_row, meta, weights, factors, block_owner, block_list, desk_owner, sems,
):
    parts = CHUNKS
    span = BLK // parts
    copies = [pltpu.make_async_copy(reduced_t, factors, sems.at[parts])]
    for part in range(parts):
        window = pl.ds(part * span, span)
        copies.append(
            pltpu.make_async_copy(loadings_t.at[:, window], weights.at[:, window], sems.at[part])
        )
    scalars = [
        pltpu.make_async_copy(block_owner_hbm, block_owner, sems.at[parts + 1]),
        pltpu.make_async_copy(block_list_hbm, block_list, sems.at[parts + 2]),
        pltpu.make_async_copy(desk_owner_hbm, desk_owner, sems.at[parts + 3]),
    ]
    later = [pltpu.make_async_copy(owner_hbm, owner_row, sems.at[parts + 4])]
    for copy in scalars + copies + later:
        copy.start()
    for copy in scalars:
        copy.wait()
    device = lax.axis_index("fac")
    live = jnp.int32(0)
    first = jnp.int32(0)
    second = jnp.int32(0)
    for block in reversed(range(block_owner.shape[0])):
        hit = block_owner[block] == device
        second = jnp.where(hit, first, second)
        first = jnp.where(hit, block, first)
        live = live + jnp.where(hit, 1, 0)
    meta[0] = live
    sources = [device]
    for slot, block in enumerate((first, second)):
        row = block_list[0, block]
        col = block_list[1, block]
        desk = block_list[2, block]
        meta[2 + 6 * slot] = block_code(row, device)
        meta[4 + 6 * slot] = block_code(col, device)
        meta[5 + 6 * slot] = desk
        meta[6 + 6 * slot] = desk_owner[desk]
        sources += [row, col]
    for index, block in enumerate(sources):
        copy = pltpu.make_async_copy(tiles_hbm.at[block], tiles.at[index], sems.at[parts + 5 + index])
        copy.start()
        later.append(copy)
    copies[0].wait()
    for part in range(parts):
        copies[1 + part].wait()
        window = pl.ds(part * span, span)
        shocks[:, window] = lax.dot_general(
            factors[...], weights[:, window], (((1,), (0,)), ((), ())),
            preferred_element_type=jnp.float32,
        ).astype(jnp.bfloat16)
    for copy in later:
        copy.wait()


def lane_row(tile):
    return jnp.concatenate([tile[q : q + 1, :] for q in range(tile.shape[0])], axis=1)


def masked_rows(shocks, bucket_tile):
    bucket = jnp.broadcast_to(lane_row(bucket_tile), shocks.shape)
    value = shocks.astype(jnp.float32)
    pieces = [jnp.where(bucket >= h, value, 0.0) for h in range(HORIZONS)]
    return jnp.concatenate(pieces, axis=0).astype(jnp.bfloat16)


def packed_tail(tail):
    count = tail.shape[0]
    row = lax.broadcasted_iota(jnp.int32, (count, 64), 0) % ROWS
    pieces = []
    for q in range(4):
        piece = jnp.where(row == DESK_DEV, pltpu.roll(tail, DESK_DEV - q, 0), 0.0)
        if q == 0:
            piece = jnp.where(row == DESK_DEV + 1, pltpu.roll(tail, DESK_DEV - 3, 0), piece)
        pieces.append(piece)
    return jnp.concatenate(pieces, axis=1)


def encoded(chunks):
    largest = jnp.max(jnp.abs(chunks), axis=1, keepdims=True)
    exponent = jnp.ceil(jnp.log2(jnp.maximum(largest, 2.0**-100))) - 14.0
    shape = chunks.shape
    exponent = jnp.broadcast_to(exponent, shape)
    row = lax.broadcasted_iota(jnp.int32, shape, 1)
    value = jnp.where(row == ROWS - 1, exponent, jnp.round(chunks * jnp.exp2(-exponent)))
    value = jnp.concatenate([value[:, :, :128], value[:, :, 128:]], axis=1)
    return value.astype(jnp.int32).astype(jnp.int16)


def delta_kernel(
    meta, own, tiles, owner_row_ref, sens_hbm, gamma_hbm, out, coded, gamma, ranks, sens_t, sems
):
    sens_copy = pltpu.make_async_copy(sens_hbm, sens_t, sems.at[0])
    copy = pltpu.make_async_copy(gamma_hbm, gamma, sems.at[1])
    sens_copy.start()
    copy.start()
    desks = sens_t.shape[0]
    fac_count = out.shape[0]
    count = fac_count * ROWS
    owner_row = owner_row_ref[...]
    groups = lax.broadcasted_iota(jnp.int32, (fac_count, desks), 0)
    member = jnp.where(groups == jnp.broadcast_to(owner_row, (fac_count, desks)), 1.0, 0.0)
    before = jnp.where(
        lax.broadcasted_iota(jnp.int32, (desks, desks), 0)
        < lax.broadcasted_iota(jnp.int32, (desks, desks), 1),
        1.0,
        0.0,
    )
    prefix = lax.dot_general(
        member.astype(jnp.bfloat16), before.astype(jnp.bfloat16), (((1,), (0,)), ((), ())),
        preferred_element_type=jnp.float32,
    )
    rank = jnp.sum(prefix * member, axis=0, keepdims=True).astype(jnp.int32)
    slot_row = owner_row * ROWS + rank
    placement = jnp.where(
        lax.broadcasted_iota(jnp.int32, (count, desks), 0)
        == jnp.broadcast_to(slot_row, (count, desks)),
        1.0,
        0.0,
    ).astype(jnp.bfloat16)
    masked = masked_rows(own[...], tiles[0])
    sens_copy.wait()
    placed = lax.dot_general(
        placement, sens_t[...], (((1,), (0,)), ((), ())), preferred_element_type=jnp.float32
    ).astype(jnp.bfloat16)
    delta = lax.dot_general(
        placed, masked, (((1,), (1,)), ((), ())), preferred_element_type=jnp.float32
    )
    packed = delta[:, :LANES] + packed_tail(delta[:, LANES:])
    chunks = packed.reshape(fac_count, ROWS, LANES)
    out[...] = chunks
    coded[...] = encoded(chunks)
    for slot in range(CAP):
        earlier = jnp.logical_and(
            owner_row == meta[6 + 6 * slot],
            lax.broadcasted_iota(jnp.int32, (1, desks), 1) < meta[5 + 6 * slot],
        )
        found = jnp.sum(jnp.where(earlier, 1.0, 0.0), axis=1, keepdims=True).astype(jnp.int32)
        ranks[slot] = jnp.broadcast_to(found, (ROWS, 128))
    copy.wait()


def picked(code, tile, own, others):
    value = own[...]
    for index, ref in others:
        value = jnp.where(code == index, ref[...], value)
    return masked_rows(value, tile)


def arrival(code):
    return jnp.where(code == FAR, 2, jnp.where(code == 4, 1, 0))


def products(meta, stage, own, others, tiles, gamma, product):
    for slot in range(CAP):
        row_code = meta[2 + 6 * slot]
        col_code = meta[4 + 6 * slot]
        row_stage = arrival(row_code)
        col_stage = arrival(col_code)
        live = slot < meta[0]
        by_row = jnp.logical_and(row_stage == stage, col_stage >= stage)

        @pl.when(jnp.logical_and(live, by_row))
        def _(slot=slot, row_code=row_code):
            part = picked(row_code, tiles[1 + 2 * slot], own, others)
            product[slot] = lax.dot_general(
                part, gamma[slot], (((1,), (0,)), ((), ())), preferred_element_type=jnp.float32
            )

        by_col = jnp.logical_and(row_stage > stage, col_stage == stage)

        @pl.when(jnp.logical_and(live, by_col))
        def _(slot=slot, col_code=col_code):
            part = picked(col_code, tiles[2 + 2 * slot], own, others)
            product[slot] = lax.dot_general(
                part, gamma[slot], (((1,), (1,)), ((), ())), preferred_element_type=jnp.float32
            )


def early_kernel(meta, own, near, chip_near, tiles, gamma, product):
    products(meta, 0, own, ((1, near), (3, chip_near)), tiles, gamma, product)


def next_kernel(meta, chip_far, tiles, gamma, before, product):
    del before
    products(meta, 1, chip_far, (), tiles, gamma, product)


def gamma_kernel(
    meta, own, near, far, chip_near, chip_far, tiles, ranks, gamma, early, delta, coded,
    out, product,
):
    del coded, early
    width = HORIZONS * own.shape[0]
    live = meta[0]
    others = ((1, near), (FAR, far), (3, chip_near), (4, chip_far))
    for slot in range(CAP):
        both = jnp.logical_and(meta[2 + 6 * slot] == FAR, meta[4 + 6 * slot] == FAR)

        @pl.when(jnp.logical_and(slot < live, both))
        def _(slot=slot):
            part = masked_rows(far[...], tiles[1 + 2 * slot])
            product[slot] = lax.dot_general(
                part, gamma[slot], (((1,), (0,)), ((), ())), preferred_element_type=jnp.float32
            )

    diagonal = lax.broadcasted_iota(jnp.int32, (width, width), 0) == lax.broadcasted_iota(
        jnp.int32, (width, width), 1
    )
    quarter = lax.broadcasted_iota(jnp.int32, (ROWS, LANES), 1) // 64
    row = lax.broadcasted_iota(jnp.int32, (ROWS, LANES), 0)
    sums = []
    for slot in range(CAP):
        row_code = meta[2 + 6 * slot]
        use_row = arrival(row_code) > arrival(meta[4 + 6 * slot])
        tile = jnp.where(use_row, tiles[1 + 2 * slot], tiles[2 + 2 * slot])
        part = picked(jnp.where(use_row, row_code, meta[4 + 6 * slot]), tile, own, others)
        quad = 0.5 * jnp.sum(part.astype(jnp.float32) * product[slot], axis=1, keepdims=True)
        quad_row = jnp.sum(
            jnp.where(diagonal, jnp.broadcast_to(quad, (width, width)), 0.0), axis=0, keepdims=True
        )
        rank = jnp.concatenate([ranks[slot]] * 2, axis=1)
        tail_row = jnp.concatenate([quad_row[:, LANES:]] * 4, axis=1)
        moved = jnp.where(rank >= 4, 4, 0)
        in_tail = jnp.logical_and(
            row == DESK_DEV + jnp.where(rank >= 4, 1, 0), quarter == rank - moved
        )
        addend = jnp.where(
            row == rank,
            jnp.broadcast_to(quad_row[:, :LANES], (ROWS, LANES)),
            jnp.where(in_tail, jnp.broadcast_to(tail_row, (ROWS, LANES)), 0.0),
        )
        sums.append(jnp.where(slot < live, addend, 0.0))
    first = meta[6]
    second = jnp.where(live > 1, meta[12], first)
    same = first == second
    one = delta[first] + sums[0] + jnp.where(same, sums[1], 0.0)
    two = delta[second] + sums[1] + jnp.where(same, sums[0], 0.0)
    out[first] = encoded(one[None])[0]
    out[second] = encoded(two[None])[0]


def sum_kernel(received, packed):
    lanes = 128
    value = received[...].astype(jnp.int32).astype(jnp.float32)
    value = value.reshape(received.shape[0] * 2, ROWS, lanes)
    scale = jnp.exp2(value[:, ROWS - 1 :, :])
    total = value * jnp.broadcast_to(scale, value.shape)
    total = jnp.sum(total.reshape(received.shape[0], 2, ROWS, lanes), axis=0)
    low, high = total[0], total[1]
    low_turned = pltpu.roll(low, 64, 1)
    high_turned = pltpu.roll(high, 64, 1)
    row = lax.broadcasted_iota(jnp.int32, (ROWS, lanes), 0)
    fifth = pltpu.roll(low, ROWS - DESK_DEV, 0)
    for j, source, shift in (
        (1, low_turned, 4), (2, high, 3), (3, high_turned, 2), (4, low, 2),
    ):
        moved = pltpu.roll(source, ROWS - shift, 0)
        fifth = jnp.where(row == j, moved, fifth)
    packed[...] = jnp.concatenate([low, high, fifth], axis=0)


def tail_kernel(
    own, other1, other2, other3, profit_hbm, shortfall_hbm, adjusted_hbm, profit, shortfall,
    adjusted, sems,
):
    copies = (
        pltpu.make_async_copy(profit, profit_hbm, sems.at[0]),
        pltpu.make_async_copy(adjusted, adjusted_hbm, sems.at[1]),
        pltpu.make_async_copy(shortfall, shortfall_hbm, sems.at[2]),
    )
    for h in range(HORIZONS):
        start = 64 * (h % 2)
        block = own[ROWS * (h // 2) : ROWS * (h // 2) + ROWS, start : start + 64]
        for j in range(DESK_DEV):
            profit[j, h : h + 1, :] = block[j : j + 1, :]
    copies[0].start()
    lanes = 128
    count = HORIZONS * ROWS
    lower = lax.broadcasted_iota(jnp.int32, (3 * ROWS, lanes), 1) < 64
    filler = jnp.zeros((lanes - count, lanes), jnp.float32)
    columns = []
    for one, two in ((own, other1), (other2, other3)):
        even = jnp.where(lower, one[...], pltpu.roll(two[...], 64, 1))
        odd = jnp.where(lower, pltpu.roll(one[...], 64, 1), two[...])
        pair = -jnp.concatenate(
            [even[:ROWS], odd[:ROWS], even[ROWS : 2 * ROWS], odd[ROWS : 2 * ROWS], even[2 * ROWS :]],
            axis=0,
        )
        columns.append(jnp.transpose(jnp.concatenate([pair, filler], axis=0)))
    values = jnp.concatenate(columns, axis=0).reshape(32, 8, lanes)
    total = jnp.zeros((1, lanes), jnp.float32)
    left = jnp.full((1, lanes), float(TAIL), jnp.float32)
    for _ in range(TAIL):
        best = jnp.max(jnp.max(values, axis=0), axis=0, keepdims=True)
        same = values == jnp.broadcast_to(best[None], values.shape)
        found = jnp.sum(jnp.sum(jnp.where(same, 1.0, 0.0), axis=0), axis=0, keepdims=True)
        taken = jnp.minimum(found, left)
        total = total + jnp.where(taken > 0.0, taken * best, 0.0)
        left = left - taken
        values = jnp.where(same, -jnp.inf, values)
    mean = jnp.broadcast_to(total * (1.0 / TAIL), (ROWS, lanes))
    row = lax.broadcasted_iota(jnp.int32, (ROWS, lanes), 0)
    by_horizon = mean
    weight = jnp.full((ROWS, lanes), horizon_weights[0], jnp.float32)
    for h in range(1, HORIZONS):
        by_horizon = jnp.where(row == h, pltpu.roll(mean, lanes - ROWS * h, 1), by_horizon)
        weight = jnp.where(row == h, horizon_weights[h], weight)
    weight = jnp.where(row < HORIZONS, weight, 0.0)
    spent = jnp.sum(weight * by_horizon * by_horizon, axis=0, keepdims=True)
    square = jnp.concatenate([by_horizon, jnp.zeros((lanes - ROWS, lanes), jnp.float32)], axis=0)
    shortfall[...] = jnp.transpose(square)[:DESK_DEV, :HORIZONS]
    adjusted[...] = jnp.sqrt(spent + 1e-06)[:, :DESK_DEV]
    for copy in copies[1:]:
        copy.start()
    for copy in copies:
        copy.wait()


VMEM = pl.BlockSpec(memory_space=pltpu.VMEM)
SMEM = pl.BlockSpec(memory_space=pltpu.SMEM)
HBM = pl.BlockSpec(memory_space=pltpu.HBM)
ORDER = (2, 1, 0)
SCEN_ORDER = (2, 3, 1)


def held(value):
    return pltpu.with_memory_space_constraint(value, pltpu.VMEM)


def resident(value):
    return pltpu.with_memory_space_constraint(value, pltpu.HBM)


def limited(mib):
    return pltpu.CompilerParams(vmem_limit_bytes=mib << 20)


def local(
    loadings, reduced_shocks, sensitivity, cross_gamma, block_list, block_owner, desk_owner, buckets
):
    fac_count = lax.axis_size("fac")
    scen_count = lax.axis_size("scen")
    factors, s_dev = reduced_shocks.shape
    desks = desk_owner.shape[0]
    f32 = jnp.float32
    bf16 = jnp.bfloat16
    i32 = jnp.int32
    tile_shape = (fac_count, 8, BLK // 8)
    shocks, tiles, owner_row, meta = pl.pallas_call(
        shocks_kernel,
        out_shape=(
            pltpu.VMEM((s_dev, BLK), bf16),
            pltpu.VMEM((1 + 2 * CAP, *tile_shape[1:]), i32),
            pltpu.VMEM((1, desks), i32),
            pltpu.SMEM((16,), i32),
        ),
        in_specs=[HBM] * 7,
        out_specs=(VMEM, VMEM, VMEM, SMEM),
        scratch_shapes=[
            pltpu.VMEM((factors, BLK), bf16),
            pltpu.VMEM((s_dev, factors), bf16),
            pltpu.SMEM(block_owner.shape, i32),
            pltpu.SMEM(block_list.shape[::-1], i32),
            pltpu.SMEM(desk_owner.shape, i32),
            pltpu.SemaphoreType.DMA((CHUNKS + 6 + 2 * CAP,)),
        ],
        name="shocks",
        compiler_params=limited(10),
    )(
        *map(
            resident,
            (
                loadings.T, reduced_shocks.T, buckets.reshape(tile_shape),
                desk_owner.reshape(1, desks), block_owner, block_list.T, desk_owner,
            ),
        )
    )
    pairs = swap_pairs(fac_count)
    moved = {}
    for index in ORDER:
        moved[index] = lax.ppermute(shocks, "fac", pairs[index])
    chunk_shape = (fac_count, ROWS, LANES)
    coded_shape = pltpu.VMEM((fac_count, 2 * ROWS, LANES // 2), jnp.int16)
    delta, coded, gamma, ranks = pl.pallas_call(
        delta_kernel,
        out_shape=(
            pltpu.VMEM(chunk_shape, f32), coded_shape, pltpu.VMEM(cross_gamma.shape, bf16),
            pltpu.VMEM((CAP, ROWS, 128), i32),
        ),
        in_specs=[SMEM] + [VMEM] * 3 + [HBM] * 2,
        out_specs=(VMEM, VMEM, VMEM, VMEM),
        scratch_shapes=[pltpu.VMEM((desks, BLK), bf16), pltpu.SemaphoreType.DMA((2,))],
        name="delta",
        compiler_params=limited(16),
    )(meta, shocks, tiles, owner_row, resident(sensitivity.T), resident(cross_gamma))
    nearby, chip_near, chip_far = (held(moved[index]) for index in range(3))
    product_shape = pltpu.VMEM((CAP, HORIZONS * s_dev, BLK), f32)
    product = pl.pallas_call(
        early_kernel,
        out_shape=product_shape,
        in_specs=[SMEM] + [VMEM] * 5,
        out_specs=VMEM,
        name="early",
        compiler_params=limited(12),
    )(meta, shocks, nearby, chip_near, tiles, gamma)
    device = lax.axis_index("fac")
    onward = jnp.where((device % 2 == 0) == (device // 2 % 2 == 0), moved[1], moved[2])
    far = held(lax.ppermute(onward, "fac", pairs[0]))
    product = pl.pallas_call(
        next_kernel,
        out_shape=product_shape,
        in_specs=[SMEM] + [VMEM] * 4,
        out_specs=VMEM,
        input_output_aliases={4: 0},
        name="next",
        compiler_params=limited(12),
    )(meta, chip_far, tiles, gamma, product)
    terms, _ = pl.pallas_call(
        gamma_kernel,
        out_shape=(coded_shape, product_shape),
        in_specs=[SMEM] + [VMEM] * 11,
        out_specs=(VMEM, VMEM),
        input_output_aliases={11: 0, 9: 1},
        name="gamma",
        compiler_params=limited(16),
    )(
        meta, shocks, nearby, far, chip_near, chip_far, tiles, ranks, gamma, product, delta,
        coded,
    )
    received = held(lax.all_to_all(terms, "fac", 0, 0, tiled=False))
    packed = pl.pallas_call(
        sum_kernel,
        out_shape=pltpu.VMEM((3 * ROWS, 128), f32),
        in_specs=[VMEM],
        out_specs=VMEM,
        name="total",
        compiler_params=limited(8),
    )(received)
    others = []
    for step in SCEN_ORDER:
        others.append(held(lax.ppermute(packed, "scen", [(i, i ^ step) for i in range(scen_count)])))
    profit, shortfall, adjusted = pl.pallas_call(
        tail_kernel,
        out_shape=(
            jax.ShapeDtypeStruct((DESK_DEV, HORIZONS, s_dev), f32),
            jax.ShapeDtypeStruct((DESK_DEV, HORIZONS), f32),
            jax.ShapeDtypeStruct((1, DESK_DEV), f32),
        ),
        in_specs=[VMEM] * scen_count,
        out_specs=(HBM, HBM, HBM),
        scratch_shapes=[
            pltpu.VMEM((DESK_DEV, HORIZONS, s_dev), f32),
            pltpu.VMEM((DESK_DEV, HORIZONS), f32),
            pltpu.VMEM((1, DESK_DEV), f32),
            pltpu.SemaphoreType.DMA((3,)),
        ],
        name="tail",
        compiler_params=limited(8),
    )(packed, *others)
    return (profit, shortfall, adjusted.reshape(DESK_DEV))


def solution(mesh):
    return jax.shard_map(
        local,
        mesh=mesh,
        in_specs=(
            P("fac", None),
            P(None, "scen"),
            P("fac", None),
            P("fac", None, None),
            P(),
            P(),
            P(),
            P(),
        ),
        out_specs=(P("fac", None, "scen"), P("fac", None), P("fac")),
        check_vma=False,
    )
```

```python
import jax
import jax.numpy as jnp
from jax import lax
from jax.experimental import pallas as pl
from jax.experimental.pallas import tpu as pltpu
from jax.sharding import PartitionSpec as P

BLK = 1024
HORIZONS = 5
CAP = 2
DESK_DEV = 5
ROWS = 8
LANES = 256
TAIL = 7
CHUNKS = 2
FAR = 2

horizon_weights = (1.0, 1.0, 2.0, 2.0, 6.0)


def swap_pairs(count):
    near, chip_near, chip_far = [], [], []
    for index in range(count):
        near.append((index, index ^ 1))
        chip, core = divmod(index, 2)
        chip_near.append((index, (chip ^ 1) * 2 + core))
        other = ((chip + 1) ^ 1) - 1
        if 0 <= other < count // 2:
            chip_far.append((index, other * 2 + core))
    return near, chip_near, chip_far


def block_code(block, device):
    offset = block - device
    side = jnp.where(device % 2 == 0, offset, -offset)
    chip_side = jnp.where((device // 2) % 2 == 0, offset, -offset)
    beside = jnp.where(side > 0, 1, 2)
    apart = jnp.where(chip_side > 0, 3, 4)
    return jnp.where(offset == 0, 0, jnp.where(jnp.abs(offset) == 1, beside, apart))


def shocks_kernel(
    loadings_t, reduced_t, tiles_hbm, owner_hbm, block_owner_hbm, block_list_hbm, desk_owner_hbm,
    shocks, tiles, owner_row, meta, weights, factors, block_owner, block_list, desk_owner, sems,
):
    parts = CHUNKS
    span = BLK // parts
    copies = [pltpu.make_async_copy(reduced_t, factors, sems.at[parts])]
    for part in range(parts):
        window = pl.ds(part * span, span)
        copies.append(
            pltpu.make_async_copy(loadings_t.at[:, window], weights.at[:, window], sems.at[part])
        )
    scalars = [
        pltpu.make_async_copy(block_owner_hbm, block_owner, sems.at[parts + 1]),
        pltpu.make_async_copy(block_list_hbm, block_list, sems.at[parts + 2]),
        pltpu.make_async_copy(desk_owner_hbm, desk_owner, sems.at[parts + 3]),
    ]
    later = [pltpu.make_async_copy(owner_hbm, owner_row, sems.at[parts + 4])]
    for copy in scalars + copies + later:
        copy.start()
    for copy in scalars:
        copy.wait()
    device = lax.axis_index("fac")
    live = jnp.int32(0)
    first = jnp.int32(0)
    second = jnp.int32(0)
    for block in reversed(range(block_owner.shape[0])):
        hit = block_owner[block] == device
        second = jnp.where(hit, first, second)
        first = jnp.where(hit, block, first)
        live = live + jnp.where(hit, 1, 0)
    meta[0] = live
    sources = [device]
    for slot, block in enumerate((first, second)):
        row = block_list[0, block]
        col = block_list[1, block]
        desk = block_list[2, block]
        meta[2 + 6 * slot] = block_code(row, device)
        meta[4 + 6 * slot] = block_code(col, device)
        meta[5 + 6 * slot] = desk
        meta[6 + 6 * slot] = desk_owner[desk]
        sources += [row, col]
    for index, block in enumerate(sources):
        copy = pltpu.make_async_copy(tiles_hbm.at[block], tiles.at[index], sems.at[parts + 5 + index])
        copy.start()
        later.append(copy)
    copies[0].wait()
    for part in range(parts):
        copies[1 + part].wait()
        window = pl.ds(part * span, span)
        shocks[:, window] = lax.dot_general(
            factors[...], weights[:, window], (((1,), (0,)), ((), ())),
            preferred_element_type=jnp.float32,
        ).astype(jnp.bfloat16)
    for copy in later:
        copy.wait()


def lane_row(tile):
    return jnp.concatenate([tile[q : q + 1, :] for q in range(tile.shape[0])], axis=1)


def masked_rows(shocks, bucket_tile):
    bucket = jnp.broadcast_to(lane_row(bucket_tile), shocks.shape)
    value = shocks.astype(jnp.float32)
    pieces = [jnp.where(bucket >= h, value, 0.0) for h in range(HORIZONS)]
    return jnp.concatenate(pieces, axis=0).astype(jnp.bfloat16)


def packed_tail(tail):
    count = tail.shape[0]
    row = lax.broadcasted_iota(jnp.int32, (count, 64), 0) % ROWS
    pieces = []
    for q in range(4):
        piece = jnp.where(row == DESK_DEV, pltpu.roll(tail, DESK_DEV - q, 0), 0.0)
        if q == 0:
            piece = jnp.where(row == DESK_DEV + 1, pltpu.roll(tail, DESK_DEV - 3, 0), piece)
        pieces.append(piece)
    return jnp.concatenate(pieces, axis=1)


def encoded(chunks):
    largest = jnp.max(jnp.abs(chunks), axis=1, keepdims=True)
    exponent = jnp.ceil(jnp.log2(jnp.maximum(largest, 2.0**-100))) - 14.0
    shape = chunks.shape
    exponent = jnp.broadcast_to(exponent, shape)
    row = lax.broadcasted_iota(jnp.int32, shape, 1)
    value = jnp.where(row == ROWS - 1, exponent, jnp.round(chunks * jnp.exp2(-exponent)))
    value = jnp.concatenate([value[:, :, :128], value[:, :, 128:]], axis=1)
    return value.astype(jnp.int32).astype(jnp.int16)


def delta_kernel(
    meta, own, tiles, owner_row_ref, sens_hbm, gamma_hbm, out, coded, gamma, ranks, sens_t, sems
):
    sens_copy = pltpu.make_async_copy(sens_hbm, sens_t, sems.at[0])
    copy = pltpu.make_async_copy(gamma_hbm, gamma, sems.at[1])
    sens_copy.start()
    copy.start()
    desks = sens_t.shape[0]
    fac_count = out.shape[0]
    count = fac_count * ROWS
    owner_row = owner_row_ref[...]
    groups = lax.broadcasted_iota(jnp.int32, (fac_count, desks), 0)
    member = jnp.where(groups == jnp.broadcast_to(owner_row, (fac_count, desks)), 1.0, 0.0)
    before = jnp.where(
        lax.broadcasted_iota(jnp.int32, (desks, desks), 0)
        < lax.broadcasted_iota(jnp.int32, (desks, desks), 1),
        1.0,
        0.0,
    )
    prefix = lax.dot_general(
        member.astype(jnp.bfloat16), before.astype(jnp.bfloat16), (((1,), (0,)), ((), ())),
        preferred_element_type=jnp.float32,
    )
    rank = jnp.sum(prefix * member, axis=0, keepdims=True).astype(jnp.int32)
    slot_row = owner_row * ROWS + rank
    placement = jnp.where(
        lax.broadcasted_iota(jnp.int32, (count, desks), 0)
        == jnp.broadcast_to(slot_row, (count, desks)),
        1.0,
        0.0,
    ).astype(jnp.bfloat16)
    masked = masked_rows(own[...], tiles[0])
    sens_copy.wait()
    placed = lax.dot_general(
        placement, sens_t[...], (((1,), (0,)), ((), ())), preferred_element_type=jnp.float32
    ).astype(jnp.bfloat16)
    delta = lax.dot_general(
        placed, masked, (((1,), (1,)), ((), ())), preferred_element_type=jnp.float32
    )
    packed = delta[:, :LANES] + packed_tail(delta[:, LANES:])
    chunks = packed.reshape(fac_count, ROWS, LANES)
    out[...] = chunks
    coded[...] = encoded(chunks)
    for slot in range(CAP):
        earlier = jnp.logical_and(
            owner_row == meta[6 + 6 * slot],
            lax.broadcasted_iota(jnp.int32, (1, desks), 1) < meta[5 + 6 * slot],
        )
        found = jnp.sum(jnp.where(earlier, 1.0, 0.0), axis=1, keepdims=True).astype(jnp.int32)
        ranks[slot] = jnp.broadcast_to(found, (ROWS, 128))
    copy.wait()


def picked(code, tile, own, others):
    value = own[...]
    for index, ref in others:
        value = jnp.where(code == index, ref[...], value)
    return masked_rows(value, tile)


def arrival(code):
    return jnp.where(code == FAR, 2, jnp.where(code == 4, 1, 0))


def products(meta, stage, own, others, tiles, gamma, product):
    for slot in range(CAP):
        row_code = meta[2 + 6 * slot]
        col_code = meta[4 + 6 * slot]
        row_stage = arrival(row_code)
        col_stage = arrival(col_code)
        live = slot < meta[0]
        by_row = jnp.logical_and(row_stage == stage, col_stage >= stage)

        @pl.when(jnp.logical_and(live, by_row))
        def _(slot=slot, row_code=row_code):
            part = picked(row_code, tiles[1 + 2 * slot], own, others)
            product[slot] = lax.dot_general(
                part, gamma[slot], (((1,), (0,)), ((), ())), preferred_element_type=jnp.float32
            )

        by_col = jnp.logical_and(row_stage > stage, col_stage == stage)

        @pl.when(jnp.logical_and(live, by_col))
        def _(slot=slot, col_code=col_code):
            part = picked(col_code, tiles[2 + 2 * slot], own, others)
            product[slot] = lax.dot_general(
                part, gamma[slot], (((1,), (1,)), ((), ())), preferred_element_type=jnp.float32
            )


def early_kernel(meta, own, near, chip_near, tiles, gamma, product):
    products(meta, 0, own, ((1, near), (3, chip_near)), tiles, gamma, product)


def next_kernel(meta, chip_far, tiles, gamma, before, product):
    del before
    products(meta, 1, chip_far, (), tiles, gamma, product)


def gamma_kernel(
    meta, own, near, far, chip_near, chip_far, tiles, ranks, gamma, early, delta, coded,
    out, product,
):
    del coded, early
    width = HORIZONS * own.shape[0]
    live = meta[0]
    others = ((1, near), (FAR, far), (3, chip_near), (4, chip_far))
    for slot in range(CAP):
        both = jnp.logical_and(meta[2 + 6 * slot] == FAR, meta[4 + 6 * slot] == FAR)

        @pl.when(jnp.logical_and(slot < live, both))
        def _(slot=slot):
            part = masked_rows(far[...], tiles[1 + 2 * slot])
            product[slot] = lax.dot_general(
                part, gamma[slot], (((1,), (0,)), ((), ())), preferred_element_type=jnp.float32
            )

    diagonal = lax.broadcasted_iota(jnp.int32, (width, width), 0) == lax.broadcasted_iota(
        jnp.int32, (width, width), 1
    )
    quarter = lax.broadcasted_iota(jnp.int32, (ROWS, LANES), 1) // 64
    row = lax.broadcasted_iota(jnp.int32, (ROWS, LANES), 0)
    sums = []
    for slot in range(CAP):
        row_code = meta[2 + 6 * slot]
        use_row = arrival(row_code) > arrival(meta[4 + 6 * slot])
        tile = jnp.where(use_row, tiles[1 + 2 * slot], tiles[2 + 2 * slot])
        part = picked(jnp.where(use_row, row_code, meta[4 + 6 * slot]), tile, own, others)
        quad = 0.5 * jnp.sum(part.astype(jnp.float32) * product[slot], axis=1, keepdims=True)
        quad_row = jnp.sum(
            jnp.where(diagonal, jnp.broadcast_to(quad, (width, width)), 0.0), axis=0, keepdims=True
        )
        rank = jnp.concatenate([ranks[slot]] * 2, axis=1)
        tail_row = jnp.concatenate([quad_row[:, LANES:]] * 4, axis=1)
        moved = jnp.where(rank >= 4, 4, 0)
        in_tail = jnp.logical_and(
            row == DESK_DEV + jnp.where(rank >= 4, 1, 0), quarter == rank - moved
        )
        addend = jnp.where(
            row == rank,
            jnp.broadcast_to(quad_row[:, :LANES], (ROWS, LANES)),
            jnp.where(in_tail, jnp.broadcast_to(tail_row, (ROWS, LANES)), 0.0),
        )
        sums.append(jnp.where(slot < live, addend, 0.0))
    first = meta[6]
    second = jnp.where(live > 1, meta[12], first)
    same = first == second
    one = delta[first] + sums[0] + jnp.where(same, sums[1], 0.0)
    two = delta[second] + sums[1] + jnp.where(same, sums[0], 0.0)
    out[first] = encoded(one[None])[0]
    out[second] = encoded(two[None])[0]


def sum_kernel(received, packed):
    lanes = 128
    value = received[...].astype(jnp.int32).astype(jnp.float32)
    value = value.reshape(received.shape[0] * 2, ROWS, lanes)
    scale = jnp.exp2(value[:, ROWS - 1 :, :])
    total = value * jnp.broadcast_to(scale, value.shape)
    total = jnp.sum(total.reshape(received.shape[0], 2, ROWS, lanes), axis=0)
    low, high = total[0], total[1]
    low_turned = pltpu.roll(low, 64, 1)
    high_turned = pltpu.roll(high, 64, 1)
    row = lax.broadcasted_iota(jnp.int32, (ROWS, lanes), 0)
    fifth = pltpu.roll(low, ROWS - DESK_DEV, 0)
    for j, source, shift in (
        (1, low_turned, 4), (2, high, 3), (3, high_turned, 2), (4, low, 2),
    ):
        moved = pltpu.roll(source, ROWS - shift, 0)
        fifth = jnp.where(row == j, moved, fifth)
    packed[...] = jnp.concatenate([low, high, fifth], axis=0)


def profit_kernel(packed, profit):
    for h in range(HORIZONS):
        start = 64 * (h % 2)
        block = packed[ROWS * (h // 2) : ROWS * (h // 2) + ROWS, start : start + 64]
        for j in range(DESK_DEV):
            profit[j, h : h + 1, :] = block[j : j + 1, :]


def tail_kernel(own, other1, other2, other3, shortfall, adjusted):
    lanes = 128
    count = HORIZONS * ROWS
    lower = lax.broadcasted_iota(jnp.int32, (3 * ROWS, lanes), 1) < 64
    filler = jnp.zeros((lanes - count, lanes), jnp.float32)
    columns = []
    for one, two in ((own, other1), (other2, other3)):
        even = jnp.where(lower, one[...], pltpu.roll(two[...], 64, 1))
        odd = jnp.where(lower, pltpu.roll(one[...], 64, 1), two[...])
        pair = -jnp.concatenate(
            [even[:ROWS], odd[:ROWS], even[ROWS : 2 * ROWS], odd[ROWS : 2 * ROWS], even[2 * ROWS :]],
            axis=0,
        )
        columns.append(jnp.transpose(jnp.concatenate([pair, filler], axis=0)))
    values = jnp.concatenate(columns, axis=0).reshape(32, 8, lanes)
    total = jnp.zeros((1, lanes), jnp.float32)
    left = jnp.full((1, lanes), float(TAIL), jnp.float32)
    for _ in range(TAIL):
        best = jnp.max(jnp.max(values, axis=0), axis=0, keepdims=True)
        same = values == jnp.broadcast_to(best[None], values.shape)
        found = jnp.sum(jnp.sum(jnp.where(same, 1.0, 0.0), axis=0), axis=0, keepdims=True)
        taken = jnp.minimum(found, left)
        total = total + jnp.where(taken > 0.0, taken * best, 0.0)
        left = left - taken
        values = jnp.where(same, -jnp.inf, values)
    mean = jnp.broadcast_to(total * (1.0 / TAIL), (ROWS, lanes))
    row = lax.broadcasted_iota(jnp.int32, (ROWS, lanes), 0)
    by_horizon = mean
    weight = jnp.full((ROWS, lanes), horizon_weights[0], jnp.float32)
    for h in range(1, HORIZONS):
        by_horizon = jnp.where(row == h, pltpu.roll(mean, lanes - ROWS * h, 1), by_horizon)
        weight = jnp.where(row == h, horizon_weights[h], weight)
    weight = jnp.where(row < HORIZONS, weight, 0.0)
    spent = jnp.sum(weight * by_horizon * by_horizon, axis=0, keepdims=True)
    adjusted[...] = jnp.sqrt(spent + 1e-06)[:, :DESK_DEV]
    square = jnp.concatenate([by_horizon, jnp.zeros((lanes - ROWS, lanes), jnp.float32)], axis=0)
    shortfall[...] = jnp.transpose(square)[:DESK_DEV, :HORIZONS]


VMEM = pl.BlockSpec(memory_space=pltpu.VMEM)
SMEM = pl.BlockSpec(memory_space=pltpu.SMEM)
HBM = pl.BlockSpec(memory_space=pltpu.HBM)
ORDER = (2, 0, 1)
SCEN_ORDER = (2, 3, 1)


def held(value):
    return pltpu.with_memory_space_constraint(value, pltpu.VMEM)


def resident(value):
    return pltpu.with_memory_space_constraint(value, pltpu.HBM)


def limited(mib):
    return pltpu.CompilerParams(vmem_limit_bytes=mib << 20)


def local(
    loadings, reduced_shocks, sensitivity, cross_gamma, block_list, block_owner, desk_owner, buckets
):
    fac_count = lax.axis_size("fac")
    scen_count = lax.axis_size("scen")
    factors, s_dev = reduced_shocks.shape
    desks = desk_owner.shape[0]
    f32 = jnp.float32
    bf16 = jnp.bfloat16
    i32 = jnp.int32
    tile_shape = (fac_count, 8, BLK // 8)
    shocks, tiles, owner_row, meta = pl.pallas_call(
        shocks_kernel,
        out_shape=(
            pltpu.VMEM((s_dev, BLK), bf16),
            pltpu.VMEM((1 + 2 * CAP, *tile_shape[1:]), i32),
            pltpu.VMEM((1, desks), i32),
            pltpu.SMEM((16,), i32),
        ),
        in_specs=[HBM] * 7,
        out_specs=(VMEM, VMEM, VMEM, SMEM),
        scratch_shapes=[
            pltpu.VMEM((factors, BLK), bf16),
            pltpu.VMEM((s_dev, factors), bf16),
            pltpu.SMEM(block_owner.shape, i32),
            pltpu.SMEM(block_list.shape[::-1], i32),
            pltpu.SMEM(desk_owner.shape, i32),
            pltpu.SemaphoreType.DMA((CHUNKS + 6 + 2 * CAP,)),
        ],
        name="shocks",
        compiler_params=limited(10),
    )(
        *map(
            resident,
            (
                loadings.T, reduced_shocks.T, buckets.reshape(tile_shape),
                desk_owner.reshape(1, desks), block_owner, block_list.T, desk_owner,
            ),
        )
    )
    pairs = swap_pairs(fac_count)
    moved = {}
    for index in ORDER:
        moved[index] = lax.ppermute(shocks, "fac", pairs[index])
    chunk_shape = (fac_count, ROWS, LANES)
    coded_shape = pltpu.VMEM((fac_count, 2 * ROWS, LANES // 2), jnp.int16)
    delta, coded, gamma, ranks = pl.pallas_call(
        delta_kernel,
        out_shape=(
            pltpu.VMEM(chunk_shape, f32), coded_shape, pltpu.VMEM(cross_gamma.shape, bf16),
            pltpu.VMEM((CAP, ROWS, 128), i32),
        ),
        in_specs=[SMEM] + [VMEM] * 3 + [HBM] * 2,
        out_specs=(VMEM, VMEM, VMEM, VMEM),
        scratch_shapes=[pltpu.VMEM((desks, BLK), bf16), pltpu.SemaphoreType.DMA((2,))],
        name="delta",
        compiler_params=limited(16),
    )(meta, shocks, tiles, owner_row, resident(sensitivity.T), resident(cross_gamma))
    nearby, chip_near, chip_far = (held(moved[index]) for index in range(3))
    product_shape = pltpu.VMEM((CAP, HORIZONS * s_dev, BLK), f32)
    product = pl.pallas_call(
        early_kernel,
        out_shape=product_shape,
        in_specs=[SMEM] + [VMEM] * 5,
        out_specs=VMEM,
        name="early",
        compiler_params=limited(12),
    )(meta, shocks, nearby, chip_near, tiles, gamma)
    device = lax.axis_index("fac")
    onward = jnp.where((device % 2 == 0) == (device // 2 % 2 == 0), moved[1], moved[2])
    far = held(lax.ppermute(onward, "fac", pairs[0]))
    product = pl.pallas_call(
        next_kernel,
        out_shape=product_shape,
        in_specs=[SMEM] + [VMEM] * 4,
        out_specs=VMEM,
        input_output_aliases={4: 0},
        name="next",
        compiler_params=limited(12),
    )(meta, chip_far, tiles, gamma, product)
    terms, _ = pl.pallas_call(
        gamma_kernel,
        out_shape=(coded_shape, product_shape),
        in_specs=[SMEM] + [VMEM] * 11,
        out_specs=(VMEM, VMEM),
        input_output_aliases={11: 0, 9: 1},
        name="gamma",
        compiler_params=limited(16),
    )(
        meta, shocks, nearby, far, chip_near, chip_far, tiles, ranks, gamma, product, delta,
        coded,
    )
    received = held(lax.all_to_all(terms, "fac", 0, 0, tiled=False))
    packed = pl.pallas_call(
        sum_kernel,
        out_shape=pltpu.VMEM((3 * ROWS, 128), f32),
        in_specs=[VMEM],
        out_specs=VMEM,
        name="total",
        compiler_params=limited(8),
    )(received)
    profit = pl.pallas_call(
        profit_kernel,
        out_shape=jax.ShapeDtypeStruct((DESK_DEV, HORIZONS, s_dev), f32),
        in_specs=[VMEM],
        out_specs=VMEM,
        name="profit",
        compiler_params=limited(4),
    )(packed)
    others = []
    for step in SCEN_ORDER:
        others.append(held(lax.ppermute(packed, "scen", [(i, i ^ step) for i in range(scen_count)])))
    shortfall, adjusted = pl.pallas_call(
        tail_kernel,
        out_shape=(
            jax.ShapeDtypeStruct((DESK_DEV, HORIZONS), f32),
            jax.ShapeDtypeStruct((1, DESK_DEV), f32),
        ),
        in_specs=[VMEM] * scen_count,
        out_specs=(VMEM, VMEM),
        name="tail",
        compiler_params=limited(8),
    )(packed, *others)
    return (profit, shortfall, adjusted.reshape(DESK_DEV))


def solution(mesh):
    return jax.shard_map(
        local,
        mesh=mesh,
        in_specs=(
            P("fac", None),
            P(None, "scen"),
            P("fac", None),
            P("fac", None, None),
            P(),
            P(),
            P(),
            P(),
        ),
        out_specs=(P("fac", None, "scen"), P("fac", None), P("fac")),
        check_vma=False,
    )
```
